32 devices in a mesh: seg: 4 (over y, core), dp: 8 (over z, x).
Axes of the slice: x: 2, y: 2, z: 4, core: 2. Of those that a mesh axis runs over, the one named last changes fastest.
Arguments:
- queries: bfloat16 [8, 512, 2048], P('dp', 'seg'), may hold values from -32 to 32
- keys: bfloat16 [8, 512, 2048], P('dp', 'seg'), may hold values from -6 to 6
- values: bfloat16 [8, 512, 2048], P('dp', 'seg'), may hold values from -6 to 6
- rel_keys: bfloat16 [256, 2048], replicated, may hold values from -6 to 6
- bias_u: float32 [2048], replicated, may hold values from -3 to 3
- bias_v: float32 [2048], replicated, may hold values from -3 to 3
- d_out: bfloat16 [8, 512, 2048], P('dp', 'seg'), may hold values from -6 to 6
Outputs:
- d_queries: bfloat16 [8, 512, 2048], P('dp', 'seg')
- d_keys: bfloat16 [8, 512, 2048], P('dp', 'seg')
- d_rel_keys: float32 [256, 2048], P('seg', 'dp')
- d_bias_u: float32 [2048], replicated
- d_bias_v: float32 [2048], replicated
The draws below stay inside these ranges and needn't reach their ends.
All inputs are finite; a program needn't handle non-finite values.
Results may differ from the reference program's by a relative error of at most 0.0068.
Values may be sent and summed in bfloat16 or wider, within the bound.
No kernel may reach another device: no remote copies, remote signals or barrier semaphores. Data moves between devices by JAX's collectives and lax.ppermute only.
A program may use at most 64 MiB of HBM per device.

```python
import jax
import jax.numpy as jnp
from jax import lax

DH = 128
SEG = 128
MEM = 128
HW = 2048
DOCS = 8
LEN = 512
N_SEG = 4


def draw_queries(key, part):
    full_shape = (DOCS, LEN, HW)
    return jnp.clip(jax.random.normal(jax.random.fold_in(key, 1), full_shape, jnp.float32), -6.0, 6.0).astype(jnp.bfloat16)


def draw_keys(key, part):
    full_shape = (DOCS, LEN, HW)
    return jnp.clip(jax.random.normal(jax.random.fold_in(key, 2), full_shape, jnp.float32), -6.0, 6.0).astype(jnp.bfloat16)


def draw_rel_keys(key, part):
    full_shape = (SEG + MEM, HW)
    return jnp.clip(jax.random.normal(jax.random.fold_in(key, 3), full_shape, jnp.float32), -6.0, 6.0).astype(jnp.bfloat16)


def level_of(key, dims, pieces, low, high):
    def one(axis_at, blocks):
        heights = jax.random.uniform(jax.random.fold_in(jax.random.fold_in(key, 6), axis_at), (blocks,), jnp.float32, low / len(pieces), high / len(pieces))
        return jnp.repeat(jnp.exp(heights), dims[axis_at] // blocks).reshape((-1,) + (1,) * (len(dims) - axis_at - 1))

    level = one(*pieces[0])
    for cut in pieces[1:]:
        level = level * one(*cut)
    return level


def gaussian(stream_key, extent, scale, bound, split=(), held_as=jnp.bfloat16):
    result = jax.random.normal(stream_key, extent, jnp.float32) * scale
    if len(split) > 0:
        result = level_of(stream_key, extent, split, -0.22, 0.18) * result
    return jnp.clip(result, min=-bound, max=bound).astype(held_as)


def setup_inputs(seed: int = 0) -> dict:
    streams_of = jax.random.split(jax.random.key(seed), 8)
    queries = draw_queries(jax.random.fold_in(streams_of[7], 71), 0)
    keys = draw_keys(jax.random.fold_in(streams_of[7], 71), 0)
    values = gaussian(streams_of[2], (DOCS, LEN, HW), 1.0, 6.0, ((0, 8), (1, 4)))
    rel_keys = draw_rel_keys(jax.random.fold_in(streams_of[7], 71), 0)
    bias_u = gaussian(streams_of[4], (HW,), 0.5, 3.0, (), jnp.float32)
    bias_v = gaussian(streams_of[5], (HW,), 0.5, 3.0, (), jnp.float32)
    d_out = gaussian(streams_of[6], (DOCS, LEN, HW), 1.0, 6.0, ((0, 8), (1, 4)))
    return {"queries": queries, "keys": keys, "values": values, "rel_keys": rel_keys, "bias_u": bias_u, "bias_v": bias_v, "d_out": d_out}


def product(form, left, right):
    return jnp.einsum(form, left.astype(jnp.float32), right.astype(jnp.float32), precision=lax.Precision.HIGHEST)

def shift_rel(raw_scores):
    head_count, seg_rows, key_count = raw_scores.shape
    padded = jnp.pad(raw_scores, ((0, 0), (0, 0), (1, 0)))
    folded = padded.reshape(head_count, key_count + 1, seg_rows)[:, 1:, :]
    return folded.reshape(head_count, seg_rows, key_count)

def local_grads(query_rows, key_local, value_local, key_memory, value_memory, rel_keys, bias_u, bias_v, d_out, mem_on):
    seg_rows = query_rows.shape[0]
    mem_len = key_memory.shape[0]
    key_count = seg_rows + mem_len
    head_count = query_rows.shape[1] // DH
    keys_all = jnp.concatenate([key_memory, key_local], 0).reshape(key_count, head_count, DH)
    values_all = jnp.concatenate([value_memory, value_local], 0).reshape(key_count, head_count, DH)
    rel_heads = rel_keys.reshape(key_count, head_count, DH)
    query_wide = query_rows.astype(jnp.float32)
    q_content = (query_wide + bias_u).astype(jnp.bfloat16).reshape(seg_rows, head_count, DH)
    q_position = (query_wide + bias_v).astype(jnp.bfloat16).reshape(seg_rows, head_count, DH)
    content = product('ihd,jhd->hij', q_content, keys_all)
    position = shift_rel(product('ihd,phd->hip', q_position, rel_heads))
    score_scale = DH ** (-0.5)
    row_index = jnp.arange(seg_rows, dtype=jnp.int32)[:, None]
    key_index = jnp.arange(key_count, dtype=jnp.int32)[None, :]
    allowed = (key_index <= row_index + mem_len) & ((key_index >= mem_len) | mem_on)
    scores = jnp.where(allowed[None], score_scale * (content + position), -1e+30)
    row_max = lax.optimization_barrier(jnp.max(scores, axis=-1, keepdims=True))
    raised = jnp.exp(scores - row_max)
    weights = raised / lax.optimization_barrier(jnp.sum(raised, axis=-1, keepdims=True))
    d_heads = d_out.reshape(seg_rows, head_count, DH)
    d_weights = product('ihd,jhd->hij', d_heads, values_all)
    centred = d_weights - lax.optimization_barrier(jnp.sum(weights * d_weights, axis=-1, keepdims=True))
    grad_scores = (score_scale * weights * centred).astype(jnp.bfloat16)
    d_content = product('hij,jhd->ihd', grad_scores, keys_all)
    d_keys = product('hij,ihd->jhd', grad_scores[:, :, mem_len:], q_content)
    zero_raw = jnp.zeros((head_count, seg_rows, key_count), jnp.bfloat16)
    unshift = jax.vjp(shift_rel, zero_raw)[1]
    grad_rel = unshift(grad_scores)[0]
    d_position = product('hip,phd->ihd', grad_rel, rel_heads)
    d_rel = product('hip,ihd->phd', grad_rel, q_position).reshape(key_count, head_count * DH)
    d_query = (d_content + d_position).reshape(seg_rows, head_count * DH).astype(jnp.bfloat16)
    d_key = d_keys.reshape(seg_rows, head_count * DH).astype(jnp.bfloat16)
    return (d_query, d_key, d_rel, lax.optimization_barrier(jnp.sum(d_content, 0)).reshape(-1), lax.optimization_barrier(jnp.sum(d_position, 0)).reshape(-1))

def reference(queries, keys, values, rel_keys, bias_u, bias_v, d_out):
    block_count = DOCS * N_SEG

    def blocks(array):
        return array.reshape(block_count, SEG, HW)

    def memory_of(array):
        split_rows = array.reshape(DOCS, N_SEG, SEG, HW)[:, :, SEG - MEM:]
        earlier = jnp.concatenate([jnp.zeros_like(split_rows[:, :1]), split_rows[:, :-1]], axis=1)
        return earlier.reshape(block_count, MEM, HW)
    seg_ids = jnp.tile(jnp.arange(N_SEG, dtype=jnp.int32), DOCS)

    def visit_block(carry, inputs):
        q_block, k_block, v_block, k_mem, v_mem, d_block, seg_id = inputs
        d_query, d_key, d_rel, d_content, d_position = local_grads(q_block, k_block, v_block, k_mem, v_mem, rel_keys, bias_u, bias_v, d_block, seg_id > 0)
        return ((carry[0] + d_rel, carry[1] + d_content, carry[2] + d_position), (d_query, d_key))
    start = (jnp.zeros((SEG + MEM, HW), jnp.float32), jnp.zeros((HW,), jnp.float32), jnp.zeros((HW,), jnp.float32))
    totals, grads = lax.scan(visit_block, start, (blocks(queries), blocks(keys), blocks(values), memory_of(keys), memory_of(values), blocks(d_out), seg_ids))
    return (grads[0].reshape(DOCS, LEN, HW), grads[1].reshape(DOCS, LEN, HW), totals[0], totals[1], totals[2])
```

```python
import jax
import jax.numpy as jnp
from jax import lax
from jax.experimental import pallas as pl
from jax.experimental.pallas import tpu as pltpu
from jax.sharding import PartitionSpec as P

DH = 128
HEADS_PER_STEP = 4
BIAS_ROWS = 16
DIRECT_PEERS = 8


def contract(left, right, left_dim, right_dim):
    return lax.dot_general(
        left,
        right,
        (((left_dim,), (right_dim,)), ((), ())),
        preferred_element_type=jnp.float32,
    )


def attention_kernel(
    q_ref,
    k_ref,
    v_ref,
    k_mem_ref,
    v_mem_ref,
    rel_ref,
    bias_u_ref,
    bias_v_ref,
    d_out_ref,
    d_q_ref,
    d_k_ref,
    keep_ref,
    send_ref,
    bias_ref,
):
    seg_rows = q_ref.shape[0]
    mem_len = k_mem_ref.shape[0]
    key_count = seg_rows + mem_len
    pair_count, part_rows, _ = keep_ref.shape
    seg_index = lax.axis_index("seg")
    first_key = jnp.where(seg_index > 0, 0, mem_len)
    odd = jnp.bitwise_and(seg_index, 1) == 1
    row_index = lax.broadcasted_iota(jnp.int32, (seg_rows, key_count), 0)
    key_index = lax.broadcasted_iota(jnp.int32, (seg_rows, key_count), 1)
    allowed = (key_index <= row_index + mem_len) & (key_index >= first_key)
    mirror_row = lax.broadcasted_iota(jnp.int32, (key_count, key_count), 0)
    mirror_col = lax.broadcasted_iota(jnp.int32, (key_count, key_count), 1)
    mirror = (mirror_row + mirror_col == key_count - 1).astype(jnp.bfloat16)
    score_scale = DH ** (-0.5)
    for head in range(q_ref.shape[1] // DH):
        cols = slice(head * DH, (head + 1) * DH)
        query_wide = q_ref[:, cols].astype(jnp.float32)
        q_content = (query_wide + bias_u_ref[:, cols]).astype(jnp.bfloat16)
        q_position = (query_wide + bias_v_ref[:, cols]).astype(jnp.bfloat16)
        keys_all = jnp.concatenate([k_mem_ref[:, cols], k_ref[:, cols]], 0)
        values_all = jnp.concatenate([v_mem_ref[:, cols], v_ref[:, cols]], 0)
        rel = rel_ref[:, cols]
        content = contract(q_content, keys_all, 1, 1)
        by_distance = contract(q_position, rel, 1, 1)
        position = pltpu.roll(by_distance, key_count - seg_rows + 1, 1, stride=1, stride_axis=0)
        scores = jnp.where(allowed, score_scale * (content + position), -1e30)
        raised = jnp.exp(scores - jnp.max(scores, axis=1, keepdims=True))
        weights = raised / jnp.sum(raised, axis=1, keepdims=True)
        d_weights = contract(d_out_ref[:, cols], values_all, 1, 1)
        centred = d_weights - jnp.sum(weights * d_weights, axis=1, keepdims=True)
        grad_scores = (score_scale * weights * centred).astype(jnp.bfloat16)
        mirrored = pltpu.roll(
            contract(grad_scores, mirror, 1, 0), key_count - seg_rows + 1, 1, stride=1, stride_axis=0
        )
        grad_rel = contract(mirrored.astype(jnp.bfloat16), mirror, 1, 0).astype(jnp.bfloat16)
        d_content = contract(grad_scores, keys_all, 1, 0)
        d_position = contract(grad_rel, rel, 1, 0)
        d_q_ref[:, cols] = (d_content + d_position).astype(jnp.bfloat16)
        d_k_ref[:, cols] = contract(grad_scores[:, mem_len:], q_content, 0, 0).astype(jnp.bfloat16)
        d_rel = contract(grad_rel, q_position, 0, 0)
        sums = jnp.concatenate(
            [jnp.sum(d_content, 0, keepdims=True), jnp.sum(d_position, 0, keepdims=True)], 0
        )
        bias_ref[:, cols] = sums
        high = sums.astype(jnp.bfloat16)
        low = (sums - high.astype(jnp.float32)).astype(jnp.bfloat16)
        fill = jnp.zeros((BIAS_ROWS - 4, DH), jnp.bfloat16)
        for pair in range(pair_count):
            start = 2 * pair * part_rows
            even_part = d_rel[start : start + part_rows]
            odd_part = d_rel[start + part_rows : start + 2 * part_rows]
            keep_ref[pair, :, cols] = jnp.where(odd, odd_part, even_part)
            send_ref[pair * part_rows : (pair + 1) * part_rows, cols] = jnp.where(
                odd, even_part, odd_part
            ).astype(jnp.bfloat16)
        send_ref[pair_count * part_rows :, cols] = jnp.concatenate([high, low, fill], 0)


def attention(queries, keys, values, key_memory, value_memory, rel_keys, bias_u, bias_v, d_out):
    seg_rows, width = queries.shape
    key_count = rel_keys.shape[0]
    seg_count = lax.axis_size("seg")
    pair_count = seg_count // 2
    part_rows = key_count // seg_count
    span = HEADS_PER_STEP * DH

    def block(rows):
        return pl.BlockSpec((rows, span), lambda step: (0, step))

    rows_in = [seg_rows] * 3 + [key_count - seg_rows] * 2 + [key_count, 1, 1, seg_rows]
    send_rows = pair_count * part_rows + BIAS_ROWS
    return pl.pallas_call(
        attention_kernel,
        name="attention_grads",
        grid=(width // span,),
        in_specs=[block(rows) for rows in rows_in],
        out_specs=[
            block(seg_rows),
            block(seg_rows),
            pl.BlockSpec((pair_count, part_rows, span), lambda step: (0, 0, step)),
            block(send_rows),
            block(2),
        ],
        out_shape=[
            jax.ShapeDtypeStruct((seg_rows, width), jnp.bfloat16),
            jax.ShapeDtypeStruct((seg_rows, width), jnp.bfloat16),
            jax.ShapeDtypeStruct((pair_count, part_rows, width), jnp.float32),
            jax.ShapeDtypeStruct((send_rows, width), jnp.bfloat16),
            jax.ShapeDtypeStruct((2, width), jnp.float32),
        ],
        compiler_params=pltpu.CompilerParams(
            dimension_semantics=("arbitrary",), vmem_limit_bytes=48 * 1024 * 1024
        ),
    )(
        queries,
        keys,
        values,
        key_memory,
        value_memory,
        rel_keys,
        bias_u[None],
        bias_v[None],
        d_out,
    )


def from_behind(block, axis, distance):
    devices = range(lax.axis_size(axis))
    route = [(i - distance, i) for i in devices if i - distance in devices]
    return lax.ppermute(block, axis, route)


def swap(block, axis, flip):
    return lax.ppermute(block, axis, [(i, i ^ flip) for i in range(lax.axis_size(axis))])


def bit_of(axis, flip):
    return (lax.axis_index(axis) // flip) % 2


def split_bias(sums):
    high = sums.astype(jnp.bfloat16)
    return high, (sums - high.astype(jnp.float32)).astype(jnp.bfloat16)


def add_packed(keep, sums, packed):
    rows = keep.shape[0] * keep.shape[1]
    partial = packed[:rows].astype(jnp.float32).reshape(keep.shape)
    halves = packed[rows : rows + 4].astype(jnp.float32)
    return keep + partial, sums + (halves[:2] + halves[2:])


def reduce_rel(keep, packed, sums):
    seg_count = lax.axis_size("seg")
    width = keep.shape[2]
    part_rows = keep.shape[1]
    partial, sums = add_packed(keep, sums, swap(packed, "seg", 1))
    flip = 2
    while flip < seg_count:
        parts = partial.reshape(partial.shape[0] // 2, 2, part_rows, width)
        mine = bit_of("seg", flip)
        keep = lax.dynamic_index_in_dim(parts, mine, 1, keepdims=False)
        other = lax.dynamic_index_in_dim(parts, 1 - mine, 1, keepdims=False)
        high, low = split_bias(sums)
        fill = jnp.zeros((BIAS_ROWS - 4, width), jnp.bfloat16)
        packed = jnp.concatenate(
            [other.astype(jnp.bfloat16).reshape(-1, width), high, low, fill], 0
        )
        partial, sums = add_packed(keep, sums, swap(packed, "seg", flip))
        flip *= 2
    partial = partial[0]
    dp_count = lax.axis_size("dp")
    flip = dp_count // 2
    while 2 * flip > DIRECT_PEERS:
        half = partial.shape[1] // 2
        mine = bit_of("dp", flip)
        keep = lax.dynamic_slice_in_dim(partial, mine * half, half, 1)
        other = lax.dynamic_slice_in_dim(partial, (1 - mine) * half, half, 1)
        partial = keep + swap(other.astype(jnp.bfloat16), "dp", flip).astype(jnp.float32)
        sums = sums + swap(sums, "dp", flip)
        flip //= 2
    peers = 2 * flip
    place = lax.axis_index("dp") % peers
    cols = partial.shape[1] // peers
    high, low = split_bias(sums)
    tail = jnp.concatenate([high.reshape(-1, cols), low.reshape(-1, cols)], 0)
    total = lax.dynamic_slice_in_dim(partial, place * cols, cols, 1)
    for distance in range(1, peers):
        other = lax.dynamic_slice_in_dim(partial, (place ^ distance) * cols, cols, 1)
        packed = jnp.concatenate([other.astype(jnp.bfloat16), tail], 0)
        packed = swap(packed, "dp", distance).astype(jnp.float32)
        total = total + packed[:part_rows]
        halves = packed[part_rows:].reshape(2, 2, width)
        sums = sums + (halves[0] + halves[1])
    return total, sums


def shards(queries, keys, values, rel_keys, bias_u, bias_v, d_out):
    seg_rows = queries.shape[1]
    mem_len = rel_keys.shape[0] - seg_rows
    key_memory = from_behind(keys[0, seg_rows - mem_len :], "seg", 1)
    value_memory = from_behind(values[0, seg_rows - mem_len :], "seg", 1)
    d_query, d_key, keep, packed, sums = attention(
        queries[0],
        keys[0],
        values[0],
        key_memory,
        value_memory,
        rel_keys,
        bias_u,
        bias_v,
        d_out[0],
    )
    total, sums = reduce_rel(keep, packed, sums)
    return (d_query[None], d_key[None], total, sums[0], sums[1])


def solution(mesh):
    placed = (
        P("dp", "seg", None),
        P("dp", "seg", None),
        P("dp", "seg", None),
        P(),
        P(),
        P(),
        P("dp", "seg", None),
    )
    return jax.shard_map(
        shards,
        mesh=mesh,
        in_specs=placed,
        out_specs=(P("dp", "seg", None), P("dp", "seg", None), P("seg", "dp"), P(), P()),
        check_vma=False,
    )
```

```python
import functools

import jax
import jax.numpy as jnp
from jax import lax
from jax.experimental import pallas as pl
from jax.experimental.pallas import tpu as pltpu
from jax.sharding import PartitionSpec as P

DH = 128
LOG2_E = 1.4426950408889634
GROUP = 4
CHUNKS = (1024, 1024)
BIAS_ROWS = 8
DIRECT_PEERS = 8


def contract(left, right, left_dim, right_dim):
    return lax.dot_general(
        left,
        right,
        (((left_dim,), (right_dim,)), ((), ())),
        preferred_element_type=jnp.float32,
    )


def attention_kernel(
    aliased,
    q_ref,
    k_ref,
    v_ref,
    k_mem_ref,
    v_mem_ref,
    rel_ref,
    bias_u_ref,
    bias_v_ref,
    d_out_ref,
    *out_refs,
):
    d_q_ref, d_k_ref, keep_ref, send_ref, bias_ref = out_refs[aliased:]

    seg_rows = q_ref.shape[0]
    mem_len = k_mem_ref.shape[0]
    key_count = seg_rows + mem_len
    pair_count, part_rows, _ = keep_ref.shape
    seg_index = lax.axis_index("seg")
    first_key = jnp.where(seg_index > 0, 0, mem_len)
    odd = jnp.bitwise_and(seg_index, 1) == 1
    row_index = lax.broadcasted_iota(jnp.int32, (seg_rows, key_count), 0)
    key_index = lax.broadcasted_iota(jnp.int32, (seg_rows, key_count), 1)
    allowed = (key_index <= row_index + mem_len) & (key_index >= first_key)

    flip_row = lax.broadcasted_iota(jnp.int32, (seg_rows, seg_rows), 0)
    flip_col = lax.broadcasted_iota(jnp.int32, (seg_rows, seg_rows), 1)
    flip = (flip_row + flip_col == seg_rows - 1).astype(jnp.bfloat16)
    score_scale = DH ** (-0.5)
    heads = range(q_ref.shape[1] // DH)
    def group_grads(group):
        cols = [slice(h * DH, (h + 1) * DH) for h in group]
        n = range(len(group))
        q_wide = [q_ref[:, c].astype(jnp.float32) for c in cols]
        q_content = [(q_wide[t] + bias_u_ref[:, cols[t]]).astype(jnp.bfloat16) for t in n]
        q_position = [(q_wide[t] + bias_v_ref[:, cols[t]]).astype(jnp.bfloat16) for t in n]
        by_distance = [contract(q_position[t], rel_ref[:, cols[t]], 1, 1) for t in n]
        keys_all = [jnp.concatenate([k_mem_ref[:, c], k_ref[:, c]], 0) for c in cols]
        content = [contract(q_content[t], keys_all[t], 1, 1) for t in n]
        position = [pltpu.roll(by_distance[t], key_count - seg_rows + 1, 1, stride=1, stride_axis=0) for t in n]
        values_all = [jnp.concatenate([v_mem_ref[:, c], v_ref[:, c]], 0) for c in cols]
        d_weights = [contract(d_out_ref[:, cols[t]], values_all[t], 1, 1) for t in n]
        scores = [jnp.where(allowed, (score_scale * LOG2_E) * (content[t] + position[t]), -1e30) for t in n]
        top = [jnp.max(s, axis=1, keepdims=True) for s in scores]
        raised = [jnp.exp2(scores[t] - top[t]) for t in n]
        total = [jnp.sum(r, axis=1, keepdims=True) for r in raised]
        cross = [jnp.sum(raised[t] * d_weights[t], axis=1, keepdims=True) for t in n]
        inverse = [1.0 / s for s in total]
        grad_scores = [((raised[t] * (score_scale * inverse[t])) * (d_weights[t] - cross[t] * inverse[t])).astype(jnp.bfloat16) for t in n]
        flipped = [contract(flip, g, 1, 0) for g in grad_scores]
        grad_rel = [pltpu.roll(f, 0, 1, stride=1, stride_axis=0).astype(jnp.bfloat16) for f in flipped]
        d_content = [contract(grad_scores[t], keys_all[t], 1, 0) for t in n]
        for t in n:
            d_k_ref[:, cols[t]] = contract(grad_scores[t][:, mem_len:], q_content[t], 0, 0).astype(jnp.bfloat16)
        q_flip = [contract(flip, q_ref[:, c], 1, 0) for c in cols]
        q_flip = [(q_flip[t] + bias_v_ref[:, cols[t]]).astype(jnp.bfloat16) for t in n]
        grad_back = [contract(flip, g, 1, 0).astype(jnp.bfloat16) for g in grad_rel]
        d_position = [contract(grad_back[t], rel_ref[:, cols[t]], 1, 0) for t in n]
        d_rel_all = [contract(grad_rel[t], q_flip[t], 0, 0) for t in n]
        for t in n:
            c = cols[t]
            d_q_ref[:, c] = (d_content[t] + d_position[t]).astype(jnp.bfloat16)
            sums = jnp.concatenate(
                [jnp.sum(d_content[t], 0, keepdims=True), jnp.sum(d_position[t], 0, keepdims=True)], 0
            )
            bias_ref[:, c] = sums
            high = sums.astype(jnp.bfloat16)
            low = (sums - high.astype(jnp.float32)).astype(jnp.bfloat16)
            fill = jnp.zeros((BIAS_ROWS - 4, DH), jnp.bfloat16)
            d_rel = d_rel_all[t]
            for pair in range(pair_count):
                start = 2 * pair * part_rows
                even_part = d_rel[start : start + part_rows]
                odd_part = d_rel[start + part_rows : start + 2 * part_rows]
                keep_ref[pair, :, c] = jnp.where(odd, odd_part, even_part)
                send_ref[pair * part_rows : (pair + 1) * part_rows, c] = jnp.where(
                    odd, even_part, odd_part
                ).astype(jnp.bfloat16)
            send_ref[pair_count * part_rows :, c] = jnp.concatenate([high, low, fill], 0)

    for first in range(0, len(heads), GROUP):
        group_grads(heads[first:first+GROUP])


def attention(start, span, grads, queries, keys, values, key_memory, value_memory, rest):
    rel_keys, bias_u, bias_v, d_out = rest
    seg_rows, width = queries.shape
    key_count = rel_keys.shape[0]
    seg_count = lax.axis_size("seg")
    pair_count = seg_count // 2
    part_rows = key_count // seg_count
    step_cols = GROUP * DH
    first = start // step_cols

    def block(rows):
        return pl.BlockSpec((rows, step_cols), lambda step: (0, first + step))

    def own(rows):
        return pl.BlockSpec((rows, step_cols), lambda step: (0, step))

    mem_len = key_count - seg_rows
    send_rows = pair_count * part_rows + BIAS_ROWS
    in_place = pl.BlockSpec(memory_space=pl.ANY)
    return pl.pallas_call(
        functools.partial(attention_kernel, len(grads)),
        name="attention_grads",
        grid=(span // step_cols,),
        in_specs=[block(seg_rows)] * 3
        + [own(mem_len)] * 2
        + [block(key_count), block(1), block(1), block(seg_rows)]
        + [in_place] * len(grads),
        out_specs=[
            block(seg_rows),
            block(seg_rows),
            pl.BlockSpec((pair_count, part_rows, step_cols), lambda step: (0, 0, step)),
            own(send_rows),
            own(2),
        ],
        out_shape=[
            jax.ShapeDtypeStruct((seg_rows, width), jnp.bfloat16),
            jax.ShapeDtypeStruct((seg_rows, width), jnp.bfloat16),
            jax.ShapeDtypeStruct((pair_count, part_rows, span), jnp.float32),
            jax.ShapeDtypeStruct((send_rows, span), jnp.bfloat16),
            jax.ShapeDtypeStruct((2, span), jnp.float32),
        ],
        input_output_aliases={9 + n: n for n in range(len(grads))},
        compiler_params=pltpu.CompilerParams(
            dimension_semantics=("arbitrary",), vmem_limit_bytes=48 * 1024 * 1024
        ),
    )(
        *(in_hbm(block) for block in (queries, keys, values)),
        key_memory,
        value_memory,
        in_hbm(rel_keys),
        bias_u[None],
        bias_v[None],
        in_hbm(d_out),
        *grads,
    )


def in_hbm(block):
    return pltpu.with_memory_space_constraint(block, pltpu.HBM)


def from_behind(block, axis, distance):
    devices = range(lax.axis_size(axis))
    route = [(i - distance, i) for i in devices if i - distance in devices]
    return lax.ppermute(block, axis, route)


def swap(block, axis, flip):
    return lax.ppermute(block, axis, [(i, i ^ flip) for i in range(lax.axis_size(axis))])


def bit_of(axis, flip):
    return (lax.axis_index(axis) // flip) % 2


def split_bias(sums):
    high = sums.astype(jnp.bfloat16)
    return high, (sums - high.astype(jnp.float32)).astype(jnp.bfloat16)


def add_packed(keep, sums, packed):
    rows = keep.shape[0] * keep.shape[1]
    partial = packed[:rows].astype(jnp.float32).reshape(keep.shape)
    halves = packed[rows : rows + 4].astype(jnp.float32)
    return keep + partial, sums + (halves[:2] + halves[2:])


def reduce_by_halves(keeps, sends, sums):
    seg_count = lax.axis_size("seg")
    got = [swap(send, "seg", 1) for send in sends]
    added = [add_packed(*part) for part in zip(keeps, sums, got)]
    partial = jnp.concatenate([part for part, _ in added], 2)
    sums = jnp.concatenate([part for _, part in added], 1)
    part_rows, width = partial.shape[1:]
    flip = 2
    while flip < seg_count:
        parts = partial.reshape(partial.shape[0] // 2, 2, part_rows, width)
        mine = bit_of("seg", flip)
        keep = lax.dynamic_index_in_dim(parts, mine, 1, keepdims=False)
        other = lax.dynamic_index_in_dim(parts, 1 - mine, 1, keepdims=False)
        high, low = split_bias(sums)
        fill = jnp.zeros((BIAS_ROWS - 4, width), jnp.bfloat16)
        packed = jnp.concatenate(
            [other.astype(jnp.bfloat16).reshape(-1, width), high, low, fill], 0
        )
        partial, sums = add_packed(keep, sums, swap(packed, "seg", flip))
        flip *= 2
    partial = partial[0]
    dp_count = lax.axis_size("dp")
    flip = dp_count // 2
    while 2 * flip > DIRECT_PEERS:
        half = partial.shape[1] // 2
        mine = bit_of("dp", flip)
        keep = lax.dynamic_slice_in_dim(partial, mine * half, half, 1)
        other = lax.dynamic_slice_in_dim(partial, (1 - mine) * half, half, 1)
        partial = keep + swap(other.astype(jnp.bfloat16), "dp", flip).astype(jnp.float32)
        sums = sums + swap(sums, "dp", flip)
        flip //= 2
    peers = 2 * flip
    place = lax.axis_index("dp") % peers
    cols = partial.shape[1] // peers
    high, low = split_bias(sums)
    tail = jnp.concatenate([high.reshape(-1, cols), low.reshape(-1, cols)], 0)
    total = lax.dynamic_slice_in_dim(partial, place * cols, cols, 1)
    for distance in range(1, peers):
        other = lax.dynamic_slice_in_dim(partial, (place ^ distance) * cols, cols, 1)
        packed = jnp.concatenate([other.astype(jnp.bfloat16), tail], 0)
        packed = swap(packed, "dp", distance).astype(jnp.float32)
        total = total + packed[:part_rows]
        halves = packed[part_rows:].reshape(2, 2, width)
        sums = sums + (halves[0] + halves[1])
    return total, sums


def split_rows(sums, width):
    rows = [
        sums[row : row + 1, col : col + width]
        for row in range(sums.shape[0])
        for col in range(0, sums.shape[1], width)
    ]
    rows = jnp.concatenate(rows, 0)
    high = rows.astype(jnp.bfloat16).astype(jnp.float32)
    return rows, jnp.concatenate([high, rows - high], 0)


def plane_kernel(chunk_count, *refs):
    keep_refs, got_refs, sum_refs = (refs[n * chunk_count : (n + 1) * chunk_count] for n in range(3))
    own_ref, sums_ref, send_y_ref, send_x_ref, send_xy_ref = refs[3 * chunk_count :]
    part_rows, width = own_ref.shape
    upper = lax.axis_index("seg") // 2 == 1
    right = lax.axis_index("dp") % 2 == 1
    cols = 2 * width // lax.axis_size("dp")
    starts = [sum(ref.shape[1] for ref in sum_refs[:n]) for n in range(chunk_count)]

    def columns(start):
        chunk = max(n for n in range(chunk_count) if starts[n] <= start)
        at = slice(start - starts[chunk], start - starts[chunk] + cols)
        parts = []
        for part in range(2):
            rows = slice(part * part_rows, (part + 1) * part_rows)
            parts.append(keep_refs[chunk][part, :, at] + got_refs[chunk][rows, at].astype(jnp.float32))
        return jnp.where(upper, parts[1], parts[0]), jnp.where(upper, parts[0], parts[1])

    for pair in range(lax.axis_size("dp") // 2):
        mine_left, other_left = columns(2 * pair * cols)
        mine_right, other_right = columns((2 * pair + 1) * cols)
        at = slice(pair * cols, (pair + 1) * cols)
        rows = slice(0, part_rows)
        own_ref[:, at] = jnp.where(right, mine_right, mine_left)
        send_x_ref[rows, at] = jnp.where(right, mine_left, mine_right).astype(jnp.bfloat16)
        send_y_ref[rows, at] = jnp.where(right, other_right, other_left).astype(jnp.bfloat16)
        send_xy_ref[rows, at] = jnp.where(right, other_left, other_right).astype(jnp.bfloat16)
    halves = [ref[2 * part_rows : 2 * part_rows + 4].astype(jnp.float32) for ref in got_refs]
    sums = [ref[...] + (half[:2] + half[2:]) for ref, half in zip(sum_refs, halves)]
    sums, tail = split_rows(jnp.concatenate(sums, 1), width)
    sums_ref[...] = sums
    for ref in (send_y_ref, send_x_ref, send_xy_ref):
        ref[part_rows:, :] = tail.astype(jnp.bfloat16)


def line_kernel(own_ref, sums_ref, *refs):
    got_refs, (total_ref, rows_ref, *send_refs) = refs[:3], refs[3:]
    part_rows, cols = total_ref.shape
    place = lax.axis_index("dp") // 2
    count = own_ref.shape[1] // cols
    blocks = []
    for n in range(count):
        at = slice(n * cols, (n + 1) * cols)
        block = own_ref[:, at]
        for ref in got_refs:
            block = block + ref[:part_rows, at].astype(jnp.float32)
        blocks.append(block)
    sums = sums_ref[...]
    for ref in got_refs:
        halves = ref[part_rows:, :].astype(jnp.float32)
        sums = sums + (halves[: sums.shape[0]] + halves[sums.shape[0] :])
    rows, tail = split_rows(sums, cols)
    rows_ref[...] = rows
    for distance, ref in zip(range(count), (total_ref, *send_refs)):
        block = blocks[distance]
        for n in range(1, count):
            block = jnp.where(place == n, blocks[n ^ distance], block)
        if distance == 0:
            ref[...] = block
        else:
            ref[:part_rows, :] = block.astype(jnp.bfloat16)
            ref[part_rows:, :] = tail.astype(jnp.bfloat16)


def whole_call(kernel, name, out_shape, *operands):
    return pl.pallas_call(
        kernel,
        name=name,
        out_shape=[jax.ShapeDtypeStruct(*shape) for shape in out_shape],
        compiler_params=pltpu.CompilerParams(vmem_limit_bytes=48 * 1024 * 1024),
    )(*operands)


def reduce_by_planes(keeps, sends, sums):
    dp_count = lax.axis_size("dp")
    got = [swap(send, "seg", 1) for send in sends]
    part_rows = keeps[0].shape[1]
    width = sum(keep.shape[2] for keep in keeps)
    half = width // 2
    tail = 2 * 2 * width // half
    send = ((part_rows + tail, half), jnp.bfloat16)
    own, plane_sums, *sends = whole_call(
        functools.partial(plane_kernel, len(keeps)),
        "plane_parts",
        [((part_rows, half), jnp.float32), ((tail // 2, half), jnp.float32), send, send, send],
        *keeps,
        *got,
        *sums,
    )
    got = [
        swap_both(sends[2], 2, 1),
        swap_both(sends[0], 2, 0),
        swap_both(sends[1], 0, 1),
    ]
    cols = width // dp_count
    tail = 2 * 2 * width // cols
    send = ((part_rows + tail, cols), jnp.bfloat16)
    peers = dp_count // 2
    total, sums, *sends = whole_call(
        line_kernel,
        "line_parts",
        [((part_rows, cols), jnp.float32), ((tail // 2, cols), jnp.float32)] + [send] * (peers - 1),
        own,
        plane_sums,
        *got,
    )
    for distance in range(1, peers):
        packed = swap(sends[distance - 1], "dp", 2 * distance).astype(jnp.float32)
        total = total + packed[:part_rows]
        sums = sums + (packed[part_rows : part_rows + tail // 2] + packed[part_rows + tail // 2 :])
    return total, sums.reshape(2, width)


def swap_both(block, seg_flip, dp_flip):
    dp_count = lax.axis_size("dp")
    route = [
        (s * dp_count + d, (s ^ seg_flip) * dp_count + (d ^ dp_flip))
        for s in range(lax.axis_size("seg"))
        for d in range(dp_count)
    ]
    return lax.ppermute(block, ("seg", "dp"), route)


def shards(queries, keys, values, rel_keys, bias_u, bias_v, d_out):
    seg_rows, width = queries.shape[1:]
    mem_len = rel_keys.shape[0] - seg_rows
    edges = [(sum(CHUNKS[:n]), span) for n, span in enumerate(CHUNKS)]
    memory = [
        [
            from_behind(block[0, seg_rows - mem_len :, start : start + span], "seg", 1)
            for block in (keys, values)
        ]
        for start, span in edges
    ]
    grads, keeps, sends, sums = (), [], [], []
    for (start, span), (key_memory, value_memory) in zip(edges, memory):
        rest = rel_keys, bias_u, bias_v, d_out[0]
        *grads, keep, send, sum_pair = attention(
            start, span, grads, queries[0], keys[0], values[0], key_memory, value_memory, rest
        )
        keeps.append(keep)
        sends.append(send)
        sums.append(sum_pair)
    planes = lax.axis_size("seg") == 4 and lax.axis_size("dp") == 8
    reduce = reduce_by_planes if planes else reduce_by_halves
    total, sums = reduce(keeps, sends, sums)
    return (grads[0][None], grads[1][None], total, sums[0], sums[1])


def solution(mesh):
    placed = (
        P("dp", "seg", None),
        P("dp", "seg", None),
        P("dp", "seg", None),
        P(),
        P(),
        P(),
        P("dp", "seg", None),
    )
    return jax.shard_map(
        shards,
        mesh=mesh,
        in_specs=placed,
        out_specs=(P("dp", "seg", None), P("dp", "seg", None), P("seg", "dp"), P(), P()),
        check_vma=False,
    )
```

```python
import functools

import jax
import jax.numpy as jnp
from jax import lax
from jax.experimental import pallas as pl
from jax.experimental.pallas import tpu as pltpu
from jax.sharding import PartitionSpec as P

DH = 128
LOG2_E = 1.4426950408889634
GROUP = 4
CHUNKS = (1024, 1024)
BIAS_ROWS = 8
DIRECT_PEERS = 8


def contract(left, right, left_dim, right_dim):
    return lax.dot_general(
        left,
        right,
        (((left_dim,), (right_dim,)), ((), ())),
        preferred_element_type=jnp.float32,
    )


def attention_kernel(
    aliased,
    q_ref,
    k_ref,
    v_ref,
    memory_ref,
    rel_ref,
    bias_u_ref,
    bias_v_ref,
    d_out_ref,
    *out_refs,
):
    d_q_ref, d_k_ref, keep_ref, send_ref, bias_ref = out_refs[aliased:]

    seg_rows = q_ref.shape[0]
    mem_len = memory_ref.shape[0] // 2
    key_count = seg_rows + mem_len
    pair_count, part_rows, _ = keep_ref.shape
    seg_index = lax.axis_index("seg")
    first_key = jnp.where(seg_index > 0, 0, mem_len)
    odd = jnp.bitwise_and(seg_index, 1) == 1
    row_index = lax.broadcasted_iota(jnp.int32, (seg_rows, key_count), 0)
    key_index = lax.broadcasted_iota(jnp.int32, (seg_rows, key_count), 1)
    allowed = (key_index <= row_index + mem_len) & (key_index >= first_key)

    flip_row = lax.broadcasted_iota(jnp.int32, (seg_rows, seg_rows), 0)
    flip_col = lax.broadcasted_iota(jnp.int32, (seg_rows, seg_rows), 1)
    flip = (flip_row + flip_col == seg_rows - 1).astype(jnp.bfloat16)
    score_scale = DH ** (-0.5)
    heads = range(q_ref.shape[1] // DH)
    def group_grads(group):
        cols = [slice(h * DH, (h + 1) * DH) for h in group]
        n = range(len(group))
        q_wide = [q_ref[:, c].astype(jnp.float32) for c in cols]
        q_content = [(q_wide[t] + bias_u_ref[:, cols[t]]).astype(jnp.bfloat16) for t in n]
        q_position = [(q_wide[t] + bias_v_ref[:, cols[t]]).astype(jnp.bfloat16) for t in n]
        by_distance = [contract(q_position[t], rel_ref[:, cols[t]], 1, 1) for t in n]
        keys_all = [jnp.concatenate([memory_ref[:mem_len, c], k_ref[:, c]], 0) for c in cols]
        content = [contract(q_content[t], keys_all[t], 1, 1) for t in n]
        position = [pltpu.roll(by_distance[t], key_count - seg_rows + 1, 1, stride=1, stride_axis=0) for t in n]
        values_all = [jnp.concatenate([memory_ref[mem_len:, c], v_ref[:, c]], 0) for c in cols]
        d_weights = [contract(d_out_ref[:, cols[t]], values_all[t], 1, 1) for t in n]
        scores = [jnp.where(allowed, (score_scale * LOG2_E) * (content[t] + position[t]), -1e30) for t in n]
        top = [jnp.max(s, axis=1, keepdims=True) for s in scores]
        raised = [jnp.exp2(scores[t] - top[t]) for t in n]
        total = [jnp.sum(r, axis=1, keepdims=True) for r in raised]
        cross = [jnp.sum(raised[t] * d_weights[t], axis=1, keepdims=True) for t in n]
        inverse = [1.0 / s for s in total]
        grad_scores = [((raised[t] * (score_scale * inverse[t])) * (d_weights[t] - cross[t] * inverse[t])).astype(jnp.bfloat16) for t in n]
        flipped = [contract(flip, g, 1, 0) for g in grad_scores]
        grad_rel = [pltpu.roll(f, 0, 1, stride=1, stride_axis=0).astype(jnp.bfloat16) for f in flipped]
        d_content = [contract(grad_scores[t], keys_all[t], 1, 0) for t in n]
        for t in n:
            d_k_ref[:, cols[t]] = contract(grad_scores[t][:, mem_len:], q_content[t], 0, 0).astype(jnp.bfloat16)
        q_flip = [contract(flip, q_ref[:, c], 1, 0) for c in cols]
        q_flip = [(q_flip[t] + bias_v_ref[:, cols[t]]).astype(jnp.bfloat16) for t in n]
        grad_back = [contract(flip, g, 1, 0).astype(jnp.bfloat16) for g in grad_rel]
        d_position = [contract(grad_back[t], rel_ref[:, cols[t]], 1, 0) for t in n]
        d_rel_all = [contract(grad_rel[t], q_flip[t], 0, 0) for t in n]
        for t in n:
            c = cols[t]
            d_q_ref[:, c] = (d_content[t] + d_position[t]).astype(jnp.bfloat16)
            sums = jnp.concatenate(
                [jnp.sum(d_content[t], 0, keepdims=True), jnp.sum(d_position[t], 0, keepdims=True)], 0
            )
            bias_ref[:, c] = sums
            high = sums.astype(jnp.bfloat16)
            low = (sums - high.astype(jnp.float32)).astype(jnp.bfloat16)
            fill = jnp.zeros((BIAS_ROWS - 4, DH), jnp.bfloat16)
            d_rel = d_rel_all[t]
            for pair in range(pair_count):
                start = 2 * pair * part_rows
                even_part = d_rel[start : start + part_rows]
                odd_part = d_rel[start + part_rows : start + 2 * part_rows]
                keep_ref[pair, :, c] = jnp.where(odd, odd_part, even_part)
                send_ref[pair * part_rows : (pair + 1) * part_rows, c] = jnp.where(
                    odd, even_part, odd_part
                ).astype(jnp.bfloat16)
            send_ref[pair_count * part_rows :, c] = jnp.concatenate([high, low, fill], 0)

    for first in range(0, len(heads), GROUP):
        group_grads(heads[first:first+GROUP])


def attention(start, span, grads, queries, keys, values, memory, rest):
    rel_keys, bias_u, bias_v, d_out = rest
    seg_rows, width = queries.shape
    key_count = rel_keys.shape[0]
    seg_count = lax.axis_size("seg")
    pair_count = seg_count // 2
    part_rows = key_count // seg_count
    step_cols = GROUP * DH
    first = start // step_cols

    def block(rows):
        return pl.BlockSpec((rows, step_cols), lambda step: (0, first + step))

    def own(rows):
        return pl.BlockSpec((rows, step_cols), lambda step: (0, step))

    mem_len = key_count - seg_rows
    send_rows = pair_count * part_rows + BIAS_ROWS
    in_place = pl.BlockSpec(memory_space=pl.ANY)
    return pl.pallas_call(
        functools.partial(attention_kernel, len(grads)),
        name="attention_grads",
        grid=(span // step_cols,),
        in_specs=[block(seg_rows)] * 3
        + [own(2 * mem_len), block(key_count), block(1), block(1), block(seg_rows)]
        + [in_place] * len(grads),
        out_specs=[
            block(seg_rows),
            block(seg_rows),
            pl.BlockSpec((pair_count, part_rows, step_cols), lambda step: (0, 0, step)),
            own(send_rows),
            own(2),
        ],
        out_shape=[
            jax.ShapeDtypeStruct((seg_rows, width), jnp.bfloat16),
            jax.ShapeDtypeStruct((seg_rows, width), jnp.bfloat16),
            jax.ShapeDtypeStruct((pair_count, part_rows, span), jnp.float32),
            jax.ShapeDtypeStruct((send_rows, span), jnp.bfloat16),
            jax.ShapeDtypeStruct((2, span), jnp.float32),
        ],
        input_output_aliases={8 + n: n for n in range(len(grads))},
        compiler_params=pltpu.CompilerParams(
            dimension_semantics=("arbitrary",), vmem_limit_bytes=48 * 1024 * 1024
        ),
    )(
        *(in_vmem(block) for block in (queries, keys, values)),
        memory,
        in_vmem(rel_keys),
        bias_u[None],
        bias_v[None],
        in_vmem(d_out),
        *grads,
    )


def in_vmem(block):
    return pltpu.with_memory_space_constraint(block, pltpu.VMEM)


def from_behind(block, axis):
    count = lax.axis_size(axis)
    return lax.ppermute(block, axis, [(i, (i + 1) % count) for i in range(count)])


def swap(block, axis, flip):
    return lax.ppermute(block, axis, [(i, i ^ flip) for i in range(lax.axis_size(axis))])


def bit_of(axis, flip):
    return (lax.axis_index(axis) // flip) % 2


def split_bias(sums):
    high = sums.astype(jnp.bfloat16)
    return high, (sums - high.astype(jnp.float32)).astype(jnp.bfloat16)


def add_packed(keep, sums, packed):
    rows = keep.shape[0] * keep.shape[1]
    partial = packed[:rows].astype(jnp.float32).reshape(keep.shape)
    halves = packed[rows : rows + 4].astype(jnp.float32)
    return keep + partial, sums + (halves[:2] + halves[2:])


def reduce_by_halves(keeps, sends, sums):
    seg_count = lax.axis_size("seg")
    got = [swap(send, "seg", 1) for send in sends]
    added = [add_packed(*part) for part in zip(keeps, sums, got)]
    partial = jnp.concatenate([part for part, _ in added], 2)
    sums = jnp.concatenate([part for _, part in added], 1)
    part_rows, width = partial.shape[1:]
    flip = 2
    while flip < seg_count:
        parts = partial.reshape(partial.shape[0] // 2, 2, part_rows, width)
        mine = bit_of("seg", flip)
        keep = lax.dynamic_index_in_dim(parts, mine, 1, keepdims=False)
        other = lax.dynamic_index_in_dim(parts, 1 - mine, 1, keepdims=False)
        high, low = split_bias(sums)
        fill = jnp.zeros((BIAS_ROWS - 4, width), jnp.bfloat16)
        packed = jnp.concatenate(
            [other.astype(jnp.bfloat16).reshape(-1, width), high, low, fill], 0
        )
        partial, sums = add_packed(keep, sums, swap(packed, "seg", flip))
        flip *= 2
    partial = partial[0]
    dp_count = lax.axis_size("dp")
    flip = dp_count // 2
    while 2 * flip > DIRECT_PEERS:
        half = partial.shape[1] // 2
        mine = bit_of("dp", flip)
        keep = lax.dynamic_slice_in_dim(partial, mine * half, half, 1)
        other = lax.dynamic_slice_in_dim(partial, (1 - mine) * half, half, 1)
        partial = keep + swap(other.astype(jnp.bfloat16), "dp", flip).astype(jnp.float32)
        sums = sums + swap(sums, "dp", flip)
        flip //= 2
    peers = 2 * flip
    place = lax.axis_index("dp") % peers
    cols = partial.shape[1] // peers
    high, low = split_bias(sums)
    tail = jnp.concatenate([high.reshape(-1, cols), low.reshape(-1, cols)], 0)
    total = lax.dynamic_slice_in_dim(partial, place * cols, cols, 1)
    for distance in range(1, peers):
        other = lax.dynamic_slice_in_dim(partial, (place ^ distance) * cols, cols, 1)
        packed = jnp.concatenate([other.astype(jnp.bfloat16), tail], 0)
        packed = swap(packed, "dp", distance).astype(jnp.float32)
        total = total + packed[:part_rows]
        halves = packed[part_rows:].reshape(2, 2, width)
        sums = sums + (halves[0] + halves[1])
    return total, sums


def split_rows(sums, width):
    rows = [
        sums[row : row + 1, col : col + width]
        for row in range(sums.shape[0])
        for col in range(0, sums.shape[1], width)
    ]
    rows = jnp.concatenate(rows, 0)
    high = rows.astype(jnp.bfloat16).astype(jnp.float32)
    return rows, jnp.concatenate([high, rows - high], 0)


def plane_kernel(chunk_count, *refs):
    keep_refs, got_refs, sum_refs = (refs[n * chunk_count : (n + 1) * chunk_count] for n in range(3))
    own_ref, sums_ref, send_y_ref, send_x_ref, send_xy_ref = refs[3 * chunk_count :]
    part_rows, width = own_ref.shape
    upper = lax.axis_index("seg") // 2 == 1
    right = lax.axis_index("dp") % 2 == 1
    cols = 2 * width // lax.axis_size("dp")
    starts = [sum(ref.shape[1] for ref in sum_refs[:n]) for n in range(chunk_count)]

    def columns(start):
        chunk = max(n for n in range(chunk_count) if starts[n] <= start)
        at = slice(start - starts[chunk], start - starts[chunk] + cols)
        parts = []
        for part in range(2):
            rows = slice(part * part_rows, (part + 1) * part_rows)
            parts.append(keep_refs[chunk][part, :, at] + got_refs[chunk][rows, at].astype(jnp.float32))
        return jnp.where(upper, parts[1], parts[0]), jnp.where(upper, parts[0], parts[1])

    for pair in range(lax.axis_size("dp") // 2):
        mine_left, other_left = columns(2 * pair * cols)
        mine_right, other_right = columns((2 * pair + 1) * cols)
        at = slice(pair * cols, (pair + 1) * cols)
        rows = slice(0, part_rows)
        own_ref[:, at] = jnp.where(right, mine_right, mine_left)
        send_x_ref[rows, at] = jnp.where(right, mine_left, mine_right).astype(jnp.bfloat16)
        send_y_ref[rows, at] = jnp.where(right, other_right, other_left).astype(jnp.bfloat16)
        send_xy_ref[rows, at] = jnp.where(right, other_left, other_right).astype(jnp.bfloat16)
    halves = [ref[2 * part_rows : 2 * part_rows + 4].astype(jnp.float32) for ref in got_refs]
    sums = [ref[...] + (half[:2] + half[2:]) for ref, half in zip(sum_refs, halves)]
    sums, tail = split_rows(jnp.concatenate(sums, 1), width)
    sums_ref[...] = sums
    for ref in (send_y_ref, send_x_ref, send_xy_ref):
        ref[part_rows:, :] = tail.astype(jnp.bfloat16)


def line_kernel(own_ref, sums_ref, *refs):
    got_refs, (total_ref, rows_ref, *send_refs) = refs[:3], refs[3:]
    part_rows, cols = total_ref.shape
    place = lax.axis_index("dp") // 2
    count = own_ref.shape[1] // cols
    blocks = []
    for n in range(count):
        at = slice(n * cols, (n + 1) * cols)
        block = own_ref[:, at]
        for ref in got_refs:
            block = block + ref[:part_rows, at].astype(jnp.float32)
        blocks.append(block)
    sums = sums_ref[...]
    for ref in got_refs:
        halves = ref[part_rows:, :].astype(jnp.float32)
        sums = sums + (halves[: sums.shape[0]] + halves[sums.shape[0] :])
    lanes = cols // 2
    half = sums.shape[0] // 2
    rows = []
    for side in (sums[:half], sums[half:]):
        pieces = [
            side[row : row + 1, col : col + lanes]
            for row in range(half)
            for col in range(0, side.shape[1], lanes)
        ]
        rows.append(jnp.concatenate(pieces, 0))
    rows = jnp.concatenate(rows, 1)
    rows_ref[...] = rows
    for distance, ref in zip(range(count), (total_ref, *send_refs)):
        block = blocks[distance]
        for n in range(1, count):
            block = jnp.where(place == n, blocks[n ^ distance], block)
        if distance == 0:
            ref[...] = block
        else:
            ref[:part_rows, :] = block.astype(jnp.bfloat16)
            ref[part_rows:, :] = rows.astype(jnp.bfloat16)


def last_kernel(total_ref, rows_ref, *refs):
    got_refs, (out_ref, bias_u_ref, bias_v_ref) = refs[:-3], refs[-3:]
    part_rows, cols = total_ref.shape
    total, rows = total_ref[...], rows_ref[...]
    for ref in got_refs:
        total = total + ref[:part_rows, :].astype(jnp.float32)
        rows = rows + ref[part_rows:, :].astype(jnp.float32)
    out_ref[...] = total
    bias_u_ref[...] = rows[:, : cols // 2]
    bias_v_ref[...] = rows[:, cols // 2 :]


def whole_call(kernel, name, out_shape, *operands):
    return pl.pallas_call(
        kernel,
        name=name,
        out_shape=[jax.ShapeDtypeStruct(*shape) for shape in out_shape],
        compiler_params=pltpu.CompilerParams(vmem_limit_bytes=48 * 1024 * 1024),
    )(*operands)


def reduce_by_planes(keeps, sends, sums):
    dp_count = lax.axis_size("dp")
    got = [swap(send, "seg", 1) for send in sends]
    part_rows = keeps[0].shape[1]
    width = sum(keep.shape[2] for keep in keeps)
    half = width // 2
    tail = 2 * 2 * width // half
    send = ((part_rows + tail, half), jnp.bfloat16)
    own, plane_sums, *sends = whole_call(
        functools.partial(plane_kernel, len(keeps)),
        "plane_parts",
        [((part_rows, half), jnp.float32), ((tail // 2, half), jnp.float32), send, send, send],
        *keeps,
        *got,
        *sums,
    )
    got = [
        swap_both(sends[2], 2, 1),
        swap_both(sends[0], 2, 0),
        swap_both(sends[1], 0, 1),
    ]
    cols = width // dp_count
    tail = 2 * width // cols
    send = ((part_rows + tail, cols), jnp.bfloat16)
    peers = dp_count // 2
    total, rows, *sends = whole_call(
        line_kernel,
        "line_parts",
        [((part_rows, cols), jnp.float32), ((tail, cols), jnp.float32)] + [send] * (peers - 1),
        own,
        plane_sums,
        *got,
    )
    got = [swap(send, "dp", 2 * distance) for distance, send in enumerate(sends, 1)]
    side = ((tail, cols // 2), jnp.float32)
    total, *sums = whole_call(
        last_kernel, "last_sums", [((part_rows, cols), jnp.float32), side, side], total, rows, *got
    )
    return total, [half.reshape(width) for half in sums]


def swap_both(block, seg_flip, dp_flip):
    dp_count = lax.axis_size("dp")
    route = [
        (s * dp_count + d, (s ^ seg_flip) * dp_count + (d ^ dp_flip))
        for s in range(lax.axis_size("seg"))
        for d in range(dp_count)
    ]
    return lax.ppermute(block, ("seg", "dp"), route)


def shards(queries, keys, values, rel_keys, bias_u, bias_v, d_out):
    seg_rows, width = queries.shape[1:]
    mem_len = rel_keys.shape[0] - seg_rows
    edges = [(sum(CHUNKS[:n]), span) for n, span in enumerate(CHUNKS)]
    memory = [
        from_behind(
            jnp.concatenate(
                [
                    block[0, seg_rows - mem_len :, start : start + span]
                    for block in (keys, values)
                ],
                0,
            ),
            "seg",
        )
        for start, span in edges
    ]
    grads, keeps, sends, sums = (), [], [], []
    for (start, span), block in zip(edges, memory):
        rest = rel_keys, bias_u, bias_v, d_out[0]
        *grads, keep, send, sum_pair = attention(
            start, span, grads, queries[0], keys[0], values[0], block, rest
        )
        keeps.append(keep)
        sends.append(send)
        sums.append(sum_pair)
    planes = lax.axis_size("seg") == 4 and lax.axis_size("dp") == 8
    reduce = reduce_by_planes if planes else reduce_by_halves
    total, sums = reduce(keeps, sends, sums)
    return (grads[0][None], grads[1][None], total, sums[0], sums[1])


def solution(mesh):
    placed = (
        P("dp", "seg", None),
        P("dp", "seg", None),
        P("dp", "seg", None),
        P(),
        P(),
        P(),
        P("dp", "seg", None),
    )
    return jax.shard_map(
        shards,
        mesh=mesh,
        in_specs=placed,
        out_specs=(P("dp", "seg", None), P("dp", "seg", None), P("seg", "dp"), P(), P()),
        check_vma=False,
    )
```

```python
import functools

import jax
import jax.numpy as jnp
from jax import lax
from jax.experimental import pallas as pl
from jax.experimental.pallas import tpu as pltpu
from jax.sharding import PartitionSpec as P

DH = 128
LOG2_E = 1.4426950408889634
GROUP = 4
CHUNKS = (1024, 1024)
VMEM_BYTES = 24 * 1024 * 1024
SCORE_SCALE = DH ** (-0.5)
BIAS_ROWS = 8
DIRECT_PEERS = 8


def contract(left, right, left_dim, right_dim):
    return lax.dot_general(
        left,
        right,
        (((left_dim,), (right_dim,)), ((), ())),
        preferred_element_type=jnp.float32,
    )


def local_kernel(q_ref, k_ref, rel_ref, bias_u_ref, bias_v_ref, score_ref, content_ref, flipped_ref):
    seg_rows = q_ref.shape[0]
    key_count = rel_ref.shape[0]
    mem_len = key_count - seg_rows
    first_key = jnp.where(lax.axis_index("seg") > 0, 0, mem_len)
    row_index = lax.broadcasted_iota(jnp.int32, (seg_rows, key_count), 0)
    key_index = lax.broadcasted_iota(jnp.int32, (seg_rows, key_count), 1)
    allowed = (key_index <= row_index + mem_len) & (key_index >= first_key)
    flip = row_flip(seg_rows)
    for group in head_groups(0, q_ref.shape[1]):
        cols = columns_of(group)
        n = range(len(cols))
        wide = [q_ref[:, c].astype(jnp.float32) for c in cols]
        q_position = [(wide[t] + bias_v_ref[:, cols[t]]).astype(jnp.bfloat16) for t in n]
        by_distance = [contract(q_position[t], rel_ref[:, cols[t]], 1, 1) for t in n]
        q_content = [(wide[t] + bias_u_ref[:, cols[t]]).astype(jnp.bfloat16) for t in n]
        content = [contract(q_content[t], k_ref[:, cols[t]], 1, 1) for t in n]
        flipped = [contract(flip, q_position[t], 1, 0).astype(jnp.bfloat16) for t in n]
        position = [
            pltpu.roll(raw, key_count - seg_rows + 1, 1, stride=1, stride_axis=0) for raw in by_distance
        ]
        for t in n:
            scores = jnp.concatenate(
                [position[t][:, :mem_len], position[t][:, mem_len:] + content[t]], 1
            )
            score_ref[group[t]] = jnp.where(allowed, SCORE_SCALE * LOG2_E * scores, -1e30)
            content_ref[:, cols[t]] = q_content[t]
            flipped_ref[:, cols[t]] = flipped[t]


def weights_kernel(score_ref, content_ref, k_mem_ref, weights_ref):
    mem_len = k_mem_ref.shape[0]
    for group in head_groups(0, content_ref.shape[1]):
        cols = columns_of(group)
        n = range(len(cols))
        content = [contract(content_ref[:, c], k_mem_ref[:, c], 1, 1) for c in cols]
        left = [score_ref[group[t], :, :mem_len] + SCORE_SCALE * LOG2_E * content[t] for t in n]
        scores = [jnp.concatenate([left[t], score_ref[group[t], :, mem_len:]], 1) for t in n]
        top = [jnp.max(score, axis=1, keepdims=True) for score in scores]
        raised = [jnp.exp2(scores[t] - top[t]) for t in n]
        total = [jnp.sum(each, axis=1, keepdims=True) for each in raised]
        for t in n:
            weights_ref[group[t]] = raised[t] * (SCORE_SCALE / total[t])


def scores_kernel(
    start,
    weights_ref,
    flipped_ref,
    k_ref,
    v_ref,
    k_mem_ref,
    v_mem_ref,
    rel_ref,
    d_out_ref,
    grad_ref,
    grad_rel_ref,
    keep_ref,
    send_ref,
    bias_ref,
):
    seg_rows = k_ref.shape[0]
    pair_count, part_rows, _ = keep_ref.shape
    odd = jnp.bitwise_and(lax.axis_index("seg"), 1) == 1
    flip = row_flip(seg_rows)
    fill = jnp.zeros((BIAS_ROWS - 4, DH), jnp.bfloat16)
    for group in head_groups(start, v_mem_ref.shape[1]):
        cols = columns_of(group)
        own = columns_of(group, start)
        n = range(len(cols))
        values_all = [
            jnp.concatenate([v_mem_ref[:, own[t]], v_ref[:, cols[t]]], 0) for t in n
        ]
        d_weights = [contract(d_out_ref[:, cols[t]], values_all[t], 1, 1) for t in n]
        scaled = [weights_ref[group[t]] * d_weights[t] for t in n]
        mean = [jnp.sum(each, axis=1, keepdims=True) * (1.0 / SCORE_SCALE) for each in scaled]
        grad = [(weights_ref[group[t]] * (d_weights[t] - mean[t])).astype(jnp.bfloat16) for t in n]
        flipped = [contract(flip, each, 1, 0) for each in grad]
        rolled = [pltpu.roll(each, 0, 1, stride=1, stride_axis=0) for each in flipped]
        grad_rel = [each.astype(jnp.bfloat16) for each in rolled]
        d_rel_all = [contract(grad_rel[t], flipped_ref[:, cols[t]], 0, 0) for t in n]
        keys_all = [jnp.concatenate([k_mem_ref[:, c], k_ref[:, c]], 0) for c in cols]
        content = [row_sum_product(flipped[t], keys_all[t]) for t in n]
        position = [row_sum_product(rolled[t], rel_ref[:, cols[t]]) for t in n]
        for t in n:
            c = own[t]
            grad_ref[group[t] - start // DH] = grad[t]
            grad_rel_ref[group[t] - start // DH] = grad_rel[t]
            sums = jnp.concatenate([content[t], position[t]], 0)
            bias_ref[:, c] = sums
            high, low = split_bias(sums)
            d_rel = d_rel_all[t]
            for pair in range(pair_count):
                at = 2 * pair * part_rows
                even_part = d_rel[at : at + part_rows]
                odd_part = d_rel[at + part_rows : at + 2 * part_rows]
                keep_ref[pair, :, c] = jnp.where(odd, odd_part, even_part)
                send_ref[pair * part_rows : (pair + 1) * part_rows, c] = jnp.where(
                    odd, even_part, odd_part
                ).astype(jnp.bfloat16)
            send_ref[pair_count * part_rows :, c] = jnp.concatenate([high, low, fill], 0)


def row_sum_product(left, right):
    rest = jnp.sum(left, 0, keepdims=True)
    parts = []
    for _ in range(3):
        part = rest.astype(jnp.bfloat16)
        rest = rest - part.astype(jnp.float32)
        parts.append(part)
    fill = jnp.zeros((5, left.shape[1]), jnp.bfloat16)
    return jnp.sum(contract(jnp.concatenate([*parts, fill], 0), right, 1, 0), 0, keepdims=True)


def rows_kernel(chunk_count, *refs):
    grad_refs, grad_rel_refs = refs[:chunk_count], refs[chunk_count : 2 * chunk_count]
    content_ref, k_ref, k_mem_ref, rel_ref, d_q_ref, d_k_ref = refs[2 * chunk_count :]
    mem_len = k_mem_ref.shape[0]
    flip = row_flip(k_ref.shape[0])
    heads = [(n, head) for n, ref in enumerate(grad_refs) for head in range(ref.shape[0])]
    for group in head_groups(0, k_ref.shape[1]):
        cols = columns_of(group)
        places = [heads[head] for head in group]
        n = range(len(cols))
        grad = [grad_refs[chunk][head] for chunk, head in places]
        back = [
            contract(flip, grad_rel_refs[chunk][head], 1, 0).astype(jnp.bfloat16)
            for chunk, head in places
        ]
        keys_all = [jnp.concatenate([k_mem_ref[:, c], k_ref[:, c]], 0) for c in cols]
        d_content = [contract(grad[t], keys_all[t], 1, 0) for t in n]
        d_key = [contract(grad[t][:, mem_len:], content_ref[:, cols[t]], 0, 0) for t in n]
        d_position = [contract(back[t], rel_ref[:, cols[t]], 1, 0) for t in n]
        for t in n:
            d_q_ref[:, cols[t]] = (d_content[t] + d_position[t]).astype(jnp.bfloat16)
            d_k_ref[:, cols[t]] = d_key[t].astype(jnp.bfloat16)


def row_flip(rows):
    row = lax.broadcasted_iota(jnp.int32, (rows, rows), 0)
    col = lax.broadcasted_iota(jnp.int32, (rows, rows), 1)
    return (row + col == rows - 1).astype(jnp.bfloat16)


def head_groups(start, span):
    heads = range(start // DH, (start + span) // DH)
    return [heads[at : at + GROUP] for at in range(0, len(heads), GROUP)]


def columns_of(heads, start=0):
    return [slice(head * DH - start, (head + 1) * DH - start) for head in heads]


def local_scores(queries, keys, rel_keys, bias_u, bias_v):
    seg_rows, width = queries.shape
    rows = ((seg_rows, width), jnp.bfloat16)
    scores = ((width // DH, seg_rows, rel_keys.shape[0]), jnp.float32)
    operands = queries, keys, rel_keys, bias_u[None], bias_v[None]
    return whole_call(local_kernel, "local_scores", [scores, rows, rows], *operands)


def soft_weights(scores, q_content, key_memory):
    shape = [(scores.shape, jnp.float32)]
    return whole_call(weights_kernel, "soft_weights", shape, scores, q_content, key_memory)[0]


def score_grads(start, span, shared, value_memory):
    weights, q_flipped, keys, values, key_memory, rel_keys, d_out = shared
    seg_count = lax.axis_size("seg")
    pair_count = seg_count // 2
    part_rows = rel_keys.shape[0] // seg_count
    grad = ((span // DH, *weights.shape[1:]), jnp.bfloat16)
    return whole_call(
        functools.partial(scores_kernel, start),
        "score_grads",
        [
            grad,
            grad,
            ((pair_count, part_rows, span), jnp.float32),
            ((pair_count * part_rows + BIAS_ROWS, span), jnp.bfloat16),
            ((2, span), jnp.float32),
        ],
        weights,
        q_flipped,
        keys,
        values,
        key_memory,
        value_memory,
        rel_keys,
        d_out,
    )


def row_grads(grads, grads_rel, q_content, keys, key_memory, rel_keys):
    rows = (keys.shape, jnp.bfloat16)
    operands = *grads, *grads_rel, q_content, keys, key_memory, rel_keys
    kernel = functools.partial(rows_kernel, len(grads))
    return whole_call(kernel, "row_grads", [rows, rows], *operands)


def in_vmem(block):
    return pltpu.with_memory_space_constraint(block, pltpu.VMEM)


def from_behind(block, axis):
    count = lax.axis_size(axis)
    return lax.ppermute(block, axis, [(i, (i + 1) % count) for i in range(count)])


def swap(block, axis, flip):
    return lax.ppermute(block, axis, [(i, i ^ flip) for i in range(lax.axis_size(axis))])


def bit_of(axis, flip):
    return (lax.axis_index(axis) // flip) % 2


def split_bias(sums):
    high = sums.astype(jnp.bfloat16)
    return high, (sums - high.astype(jnp.float32)).astype(jnp.bfloat16)


def add_packed(keep, sums, packed):
    rows = keep.shape[0] * keep.shape[1]
    partial = packed[:rows].astype(jnp.float32).reshape(keep.shape)
    halves = packed[rows : rows + 4].astype(jnp.float32)
    return keep + partial, sums + (halves[:2] + halves[2:])


def reduce_by_halves(keeps, sends, sums):
    seg_count = lax.axis_size("seg")
    got = [swap(send, "seg", 1) for send in sends]
    added = [add_packed(*part) for part in zip(keeps, sums, got)]
    partial = jnp.concatenate([part for part, _ in added], 2)
    sums = jnp.concatenate([part for _, part in added], 1)
    part_rows, width = partial.shape[1:]
    flip = 2
    while flip < seg_count:
        parts = partial.reshape(partial.shape[0] // 2, 2, part_rows, width)
        mine = bit_of("seg", flip)
        keep = lax.dynamic_index_in_dim(parts, mine, 1, keepdims=False)
        other = lax.dynamic_index_in_dim(parts, 1 - mine, 1, keepdims=False)
        high, low = split_bias(sums)
        fill = jnp.zeros((BIAS_ROWS - 4, width), jnp.bfloat16)
        packed = jnp.concatenate(
            [other.astype(jnp.bfloat16).reshape(-1, width), high, low, fill], 0
        )
        partial, sums = add_packed(keep, sums, swap(packed, "seg", flip))
        flip *= 2
    partial = partial[0]
    dp_count = lax.axis_size("dp")
    flip = dp_count // 2
    while 2 * flip > DIRECT_PEERS:
        half = partial.shape[1] // 2
        mine = bit_of("dp", flip)
        keep = lax.dynamic_slice_in_dim(partial, mine * half, half, 1)
        other = lax.dynamic_slice_in_dim(partial, (1 - mine) * half, half, 1)
        partial = keep + swap(other.astype(jnp.bfloat16), "dp", flip).astype(jnp.float32)
        sums = sums + swap(sums, "dp", flip)
        flip //= 2
    peers = 2 * flip
    place = lax.axis_index("dp") % peers
    cols = partial.shape[1] // peers
    high, low = split_bias(sums)
    tail = jnp.concatenate([high.reshape(-1, cols), low.reshape(-1, cols)], 0)
    total = lax.dynamic_slice_in_dim(partial, place * cols, cols, 1)
    for distance in range(1, peers):
        other = lax.dynamic_slice_in_dim(partial, (place ^ distance) * cols, cols, 1)
        packed = jnp.concatenate([other.astype(jnp.bfloat16), tail], 0)
        packed = swap(packed, "dp", distance).astype(jnp.float32)
        total = total + packed[:part_rows]
        halves = packed[part_rows:].reshape(2, 2, width)
        sums = sums + (halves[0] + halves[1])
    return total, sums


def split_rows(sums, width):
    rows = [
        sums[row : row + 1, col : col + width]
        for row in range(sums.shape[0])
        for col in range(0, sums.shape[1], width)
    ]
    rows = jnp.concatenate(rows, 0)
    high = rows.astype(jnp.bfloat16).astype(jnp.float32)
    return rows, jnp.concatenate([high, rows - high], 0)


def plane_kernel(chunk_count, *refs):
    keep_refs, got_refs, sum_refs = (refs[n * chunk_count : (n + 1) * chunk_count] for n in range(3))
    own_ref, sums_ref, send_y_ref, send_x_ref, send_xy_ref = refs[3 * chunk_count :]
    part_rows, width = own_ref.shape
    upper = lax.axis_index("seg") // 2 == 1
    right = lax.axis_index("dp") % 2 == 1
    cols = 2 * width // lax.axis_size("dp")
    starts = [sum(ref.shape[1] for ref in sum_refs[:n]) for n in range(chunk_count)]

    def columns(start):
        chunk = max(n for n in range(chunk_count) if starts[n] <= start)
        at = slice(start - starts[chunk], start - starts[chunk] + cols)
        parts = []
        for part in range(2):
            rows = slice(part * part_rows, (part + 1) * part_rows)
            parts.append(keep_refs[chunk][part, :, at] + got_refs[chunk][rows, at].astype(jnp.float32))
        return jnp.where(upper, parts[1], parts[0]), jnp.where(upper, parts[0], parts[1])

    for pair in range(lax.axis_size("dp") // 2):
        mine_left, other_left = columns(2 * pair * cols)
        mine_right, other_right = columns((2 * pair + 1) * cols)
        at = slice(pair * cols, (pair + 1) * cols)
        rows = slice(0, part_rows)
        own_ref[:, at] = jnp.where(right, mine_right, mine_left)
        send_x_ref[rows, at] = jnp.where(right, mine_left, mine_right).astype(jnp.bfloat16)
        send_y_ref[rows, at] = jnp.where(right, other_right, other_left).astype(jnp.bfloat16)
        send_xy_ref[rows, at] = jnp.where(right, other_left, other_right).astype(jnp.bfloat16)
    halves = [ref[2 * part_rows : 2 * part_rows + 4].astype(jnp.float32) for ref in got_refs]
    sums = [ref[...] + (half[:2] + half[2:]) for ref, half in zip(sum_refs, halves)]
    sums, tail = split_rows(jnp.concatenate(sums, 1), width)
    sums_ref[...] = sums
    for ref in (send_y_ref, send_x_ref, send_xy_ref):
        ref[part_rows:, :] = tail.astype(jnp.bfloat16)


def line_kernel(own_ref, sums_ref, *refs):
    got_refs, (total_ref, rows_ref, *send_refs) = refs[:3], refs[3:]
    part_rows, cols = total_ref.shape
    place = lax.axis_index("dp") // 2
    count = own_ref.shape[1] // cols
    blocks = []
    for n in range(count):
        at = slice(n * cols, (n + 1) * cols)
        block = own_ref[:, at]
        for ref in got_refs:
            block = block + ref[:part_rows, at].astype(jnp.float32)
        blocks.append(block)
    sums = sums_ref[...]
    for ref in got_refs:
        halves = ref[part_rows:, :].astype(jnp.float32)
        sums = sums + (halves[: sums.shape[0]] + halves[sums.shape[0] :])
    lanes = cols // 2
    half = sums.shape[0] // 2
    rows = []
    for side in (sums[:half], sums[half:]):
        pieces = [
            side[row : row + 1, col : col + lanes]
            for row in range(half)
            for col in range(0, side.shape[1], lanes)
        ]
        rows.append(jnp.concatenate(pieces, 0))
    rows = jnp.concatenate(rows, 1)
    rows_ref[...] = rows
    for distance, ref in zip(range(count), (total_ref, *send_refs)):
        block = blocks[distance]
        for n in range(1, count):
            block = jnp.where(place == n, blocks[n ^ distance], block)
        if distance == 0:
            ref[...] = block
        else:
            ref[:part_rows, :] = block.astype(jnp.bfloat16)
            ref[part_rows:, :] = rows.astype(jnp.bfloat16)


def last_kernel(total_ref, rows_ref, *refs):
    got_refs, (out_ref, bias_u_ref, bias_v_ref) = refs[:-3], refs[-3:]
    part_rows, cols = total_ref.shape
    total, rows = total_ref[...], rows_ref[...]
    for ref in got_refs:
        total = total + ref[:part_rows, :].astype(jnp.float32)
        rows = rows + ref[part_rows:, :].astype(jnp.float32)
    out_ref[...] = total
    bias_u_ref[...] = rows[:, : cols // 2]
    bias_v_ref[...] = rows[:, cols // 2 :]


def whole_call(kernel, name, out_shape, *operands):
    return pl.pallas_call(
        kernel,
        name=name,
        out_shape=[jax.ShapeDtypeStruct(*shape) for shape in out_shape],
        compiler_params=pltpu.CompilerParams(vmem_limit_bytes=VMEM_BYTES),
    )(*operands)


def reduce_by_planes(keeps, sends, sums):
    dp_count = lax.axis_size("dp")
    got = [swap(send, "seg", 1) for send in sends]
    part_rows = keeps[0].shape[1]
    width = sum(keep.shape[2] for keep in keeps)
    half = width // 2
    tail = 2 * 2 * width // half
    send = ((part_rows + tail, half), jnp.bfloat16)
    own, plane_sums, *sends = whole_call(
        functools.partial(plane_kernel, len(keeps)),
        "plane_parts",
        [((part_rows, half), jnp.float32), ((tail // 2, half), jnp.float32), send, send, send],
        *keeps,
        *got,
        *sums,
    )
    got = [
        swap_both(sends[2], 2, 1),
        swap_both(sends[0], 2, 0),
        swap_both(sends[1], 0, 1),
    ]
    cols = width // dp_count
    tail = 2 * width // cols
    send = ((part_rows + tail, cols), jnp.bfloat16)
    peers = dp_count // 2
    total, rows, *sends = whole_call(
        line_kernel,
        "line_parts",
        [((part_rows, cols), jnp.float32), ((tail, cols), jnp.float32)] + [send] * (peers - 1),
        own,
        plane_sums,
        *got,
    )
    got = [swap(send, "dp", 2 * distance) for distance, send in enumerate(sends, 1)]
    side = ((tail, cols // 2), jnp.float32)
    total, *sums = whole_call(
        last_kernel, "last_sums", [((part_rows, cols), jnp.float32), side, side], total, rows, *got
    )
    return total, [half.reshape(width) for half in sums]


def swap_both(block, seg_flip, dp_flip):
    dp_count = lax.axis_size("dp")
    route = [
        (s * dp_count + d, (s ^ seg_flip) * dp_count + (d ^ dp_flip))
        for s in range(lax.axis_size("seg"))
        for d in range(dp_count)
    ]
    return lax.ppermute(block, ("seg", "dp"), route)


def shards(queries, keys, values, rel_keys, bias_u, bias_v, d_out):
    seg_rows, width = queries.shape[1:]
    mem_len = rel_keys.shape[0] - seg_rows
    edges = [(sum(CHUNKS[:n]), span) for n, span in enumerate(CHUNKS)]
    key_memory = from_behind(keys[0, seg_rows - mem_len :], "seg")
    value_memory = [
        from_behind(values[0, seg_rows - mem_len :, start : start + span], "seg")
        for start, span in edges
    ]
    own_q, own_k, own_v, rel_keys, own_d = (
        in_vmem(block) for block in (queries[0], keys[0], values[0], rel_keys, d_out[0])
    )
    scores, q_content, q_flipped = local_scores(own_q, own_k, rel_keys, bias_u, bias_v)
    weights = soft_weights(scores, q_content, key_memory)
    shared = weights, q_flipped, own_k, own_v, key_memory, rel_keys, own_d
    parts = [
        score_grads(start, span, shared, block) for (start, span), block in zip(edges, value_memory)
    ]
    grads, grads_rel, keeps, sends, sums = zip(*parts)
    planes = lax.axis_size("seg") == 4 and lax.axis_size("dp") == 8
    reduce = reduce_by_planes if planes else reduce_by_halves
    total, sums = reduce(keeps, sends, sums)
    d_query, d_key = row_grads(grads, grads_rel, q_content, own_k, key_memory, rel_keys)
    return (d_query[None], d_key[None], total, sums[0], sums[1])


def solution(mesh):
    placed = (
        P("dp", "seg", None),
        P("dp", "seg", None),
        P("dp", "seg", None),
        P(),
        P(),
        P(),
        P("dp", "seg", None),
    )
    return jax.shard_map(
        shards,
        mesh=mesh,
        in_specs=placed,
        out_specs=(P("dp", "seg", None), P("dp", "seg", None), P("seg", "dp"), P(), P()),
        check_vma=False,
    )
```

```python
import functools

import jax
import jax.numpy as jnp
from jax import lax
from jax.experimental import pallas as pl
from jax.experimental.pallas import tpu as pltpu
from jax.sharding import PartitionSpec as P

DH = 128
LOG2_E = 1.4426950408889634
GROUP = 4
CHUNKS = (768, 768, 512)
VMEM_BYTES = 24 * 1024 * 1024
SCORE_SCALE = DH ** (-0.5)
BIAS_ROWS = 8
DIRECT_PEERS = 8


def contract(left, right, left_dim, right_dim):
    return lax.dot_general(
        left,
        right,
        (((left_dim,), (right_dim,)), ((), ())),
        preferred_element_type=jnp.float32,
    )


def local_kernel(
    q_hbm,
    k_hbm,
    rel_hbm,
    v_hbm,
    d_out_hbm,
    bias_u_hbm,
    bias_v_hbm,
    score_ref,
    content_ref,
    flipped_ref,
    k_ref,
    rel_ref,
    v_ref,
    d_out_ref,
    q_ref,
    bias_u_ref,
    bias_v_ref,
    head_sems,
    bias_sems,
    rest_sems,
):
    seg_rows, width = q_ref.shape
    key_count = rel_ref.shape[0]
    mem_len = key_count - seg_rows
    groups = head_groups(0, width)
    pairs = (q_hbm, q_ref), (rel_hbm, rel_ref), (k_hbm, k_ref)
    biases = [
        pltpu.make_async_copy(bias_u_hbm, bias_u_ref, bias_sems.at[0]),
        pltpu.make_async_copy(bias_v_hbm, bias_v_ref, bias_sems.at[1]),
    ]
    copies = []
    for n, group in enumerate(groups):
        span = pl.ds(group[0] * DH, len(group) * DH)
        copies.append(
            [
                pltpu.make_async_copy(src.at[:, span], dst.at[:, span], head_sems.at[n, at])
                for at, (src, dst) in enumerate(pairs)
            ]
        )
    rest = [
        pltpu.make_async_copy(v_hbm, v_ref, rest_sems.at[0]),
        pltpu.make_async_copy(d_out_hbm, d_out_ref, rest_sems.at[1]),
    ]
    copies[0] = biases + copies[0]
    for copy in [each for part in copies for each in part] + rest:
        copy.start()
    first_key = jnp.where(lax.axis_index("seg") > 0, 0, mem_len)
    row_index = lax.broadcasted_iota(jnp.int32, (seg_rows, key_count), 0)
    key_index = lax.broadcasted_iota(jnp.int32, (seg_rows, key_count), 1)
    allowed = (key_index <= row_index + mem_len) & (key_index >= first_key)
    flip = row_flip(seg_rows)
    for group, part in zip(groups, copies):
        for copy in part:
            copy.wait()
        cols = columns_of(group)
        n = range(len(cols))
        wide = [q_ref[:, c].astype(jnp.float32) for c in cols]
        q_position = [(wide[t] + bias_v_ref[:, cols[t]]).astype(jnp.bfloat16) for t in n]
        by_distance = [contract(q_position[t], rel_ref[:, cols[t]], 1, 1) for t in n]
        q_content = [(wide[t] + bias_u_ref[:, cols[t]]).astype(jnp.bfloat16) for t in n]
        content = [contract(q_content[t], k_ref[:, cols[t]], 1, 1) for t in n]
        flipped = [contract(flip, q_position[t], 1, 0).astype(jnp.bfloat16) for t in n]
        position = [
            pltpu.roll(raw, key_count - seg_rows + 1, 1, stride=1, stride_axis=0)
            for raw in by_distance
        ]
        for t in n:
            scores = jnp.concatenate(
                [position[t][:, :mem_len], position[t][:, mem_len:] + content[t]], 1
            )
            score_ref[group[t]] = jnp.where(allowed, SCORE_SCALE * LOG2_E * scores, -1e30)
            content_ref[:, cols[t]] = q_content[t]
            flipped_ref[:, cols[t]] = flipped[t]
    for copy in rest:
        copy.wait()


def weights_kernel(score_ref, content_ref, k_mem_ref, weights_ref):
    mem_len = k_mem_ref.shape[0]
    for group in head_groups(0, content_ref.shape[1]):
        cols = columns_of(group)
        n = range(len(cols))
        content = [contract(content_ref[:, c], k_mem_ref[:, c], 1, 1) for c in cols]
        left = [score_ref[group[t], :, :mem_len] + SCORE_SCALE * LOG2_E * content[t] for t in n]
        scores = [jnp.concatenate([left[t], score_ref[group[t], :, mem_len:]], 1) for t in n]
        top = [jnp.max(score, axis=1, keepdims=True) for score in scores]
        raised = [jnp.exp2(scores[t] - top[t]) for t in n]
        total = [jnp.sum(each, axis=1, keepdims=True) for each in raised]
        for t in n:
            weights_ref[group[t]] = raised[t] * (SCORE_SCALE / total[t])


def scores_kernel(
    start,
    weights_ref,
    flipped_ref,
    k_ref,
    v_ref,
    k_mem_ref,
    v_mem_ref,
    rel_ref,
    d_out_ref,
    grad_ref,
    grad_rel_ref,
    keep_ref,
    send_ref,
    bias_ref,
):
    seg_rows = k_ref.shape[0]
    pair_count, part_rows, _ = keep_ref.shape
    odd = jnp.bitwise_and(lax.axis_index("seg"), 1) == 1
    flip = row_flip(seg_rows)
    fill = jnp.zeros((BIAS_ROWS - 4, DH), jnp.bfloat16)
    for group in head_groups(start, v_mem_ref.shape[1]):
        cols = columns_of(group)
        own = columns_of(group, start)
        n = range(len(cols))
        values_all = [
            jnp.concatenate([v_mem_ref[:, own[t]], v_ref[:, cols[t]]], 0) for t in n
        ]
        d_weights = [contract(d_out_ref[:, cols[t]], values_all[t], 1, 1) for t in n]
        scaled = [weights_ref[group[t]] * d_weights[t] for t in n]
        mean = [jnp.sum(each, axis=1, keepdims=True) * (1.0 / SCORE_SCALE) for each in scaled]
        grad = [(weights_ref[group[t]] * (d_weights[t] - mean[t])).astype(jnp.bfloat16) for t in n]
        flipped = [contract(flip, each, 1, 0) for each in grad]
        rolled = [pltpu.roll(each, 0, 1, stride=1, stride_axis=0) for each in flipped]
        grad_rel = [each.astype(jnp.bfloat16) for each in rolled]
        d_rel_all = [contract(grad_rel[t], flipped_ref[:, cols[t]], 0, 0) for t in n]
        keys_all = [jnp.concatenate([k_mem_ref[:, c], k_ref[:, c]], 0) for c in cols]
        content = [row_sum_product(flipped[t], keys_all[t]) for t in n]
        position = [row_sum_product(rolled[t], rel_ref[:, cols[t]]) for t in n]
        for t in n:
            c = own[t]
            grad_ref[group[t] - start // DH] = grad[t]
            grad_rel_ref[group[t] - start // DH] = grad_rel[t]
            sums = jnp.concatenate([content[t], position[t]], 0)
            bias_ref[:, c] = sums
            high, low = split_bias(sums)
            d_rel = d_rel_all[t]
            for pair in range(pair_count):
                at = 2 * pair * part_rows
                even_part = d_rel[at : at + part_rows]
                odd_part = d_rel[at + part_rows : at + 2 * part_rows]
                keep_ref[pair, :, c] = jnp.where(odd, odd_part, even_part)
                send_ref[pair * part_rows : (pair + 1) * part_rows, c] = jnp.where(
                    odd, even_part, odd_part
                ).astype(jnp.bfloat16)
            send_ref[pair_count * part_rows :, c] = jnp.concatenate([high, low, fill], 0)


def row_sum_product(left, right):
    rest = jnp.sum(left, 0, keepdims=True)
    parts = []
    for _ in range(3):
        part = rest.astype(jnp.bfloat16)
        rest = rest - part.astype(jnp.float32)
        parts.append(part)
    fill = jnp.zeros((5, left.shape[1]), jnp.bfloat16)
    return jnp.sum(contract(jnp.concatenate([*parts, fill], 0), right, 1, 0), 0, keepdims=True)


def rows_kernel(chunk_count, *refs):
    grad_refs, grad_rel_refs = refs[:chunk_count], refs[chunk_count : 2 * chunk_count]
    content_ref, k_ref, k_mem_ref, rel_ref, d_q_ref, d_k_ref = refs[2 * chunk_count :]
    mem_len = k_mem_ref.shape[0]
    flip = row_flip(k_ref.shape[0])
    heads = [(n, head) for n, ref in enumerate(grad_refs) for head in range(ref.shape[0])]
    for group in head_groups(0, k_ref.shape[1]):
        cols = columns_of(group)
        places = [heads[head] for head in group]
        n = range(len(cols))
        grad = [grad_refs[chunk][head] for chunk, head in places]
        back = [
            contract(flip, grad_rel_refs[chunk][head], 1, 0).astype(jnp.bfloat16)
            for chunk, head in places
        ]
        keys_all = [jnp.concatenate([k_mem_ref[:, c], k_ref[:, c]], 0) for c in cols]
        d_content = [contract(grad[t], keys_all[t], 1, 0) for t in n]
        d_key = [contract(grad[t][:, mem_len:], content_ref[:, cols[t]], 0, 0) for t in n]
        d_position = [contract(back[t], rel_ref[:, cols[t]], 1, 0) for t in n]
        for t in n:
            d_q_ref[:, cols[t]] = (d_content[t] + d_position[t]).astype(jnp.bfloat16)
            d_k_ref[:, cols[t]] = d_key[t].astype(jnp.bfloat16)


def row_flip(rows):
    row = lax.broadcasted_iota(jnp.int32, (rows, rows), 0)
    col = lax.broadcasted_iota(jnp.int32, (rows, rows), 1)
    return (row + col == rows - 1).astype(jnp.bfloat16)


def head_groups(start, span):
    heads = range(start // DH, (start + span) // DH)
    size = GROUP if len(heads) % GROUP == 0 else len(heads)
    return [heads[at : at + size] for at in range(0, len(heads), size)]


def columns_of(heads, start=0):
    return [slice(head * DH - start, (head + 1) * DH - start) for head in heads]


def local_scores(queries, keys, rel_keys, values, d_out, bias_u, bias_v):
    seg_rows, width = queries.shape
    rows = jax.ShapeDtypeStruct((seg_rows, width), jnp.bfloat16)
    groups = len(head_groups(0, width))
    scores = jax.ShapeDtypeStruct((width // DH, seg_rows, rel_keys.shape[0]), jnp.float32)
    rel = jax.ShapeDtypeStruct(rel_keys.shape, jnp.bfloat16)
    stays = pl.BlockSpec(memory_space=pl.ANY)
    whole = pl.BlockSpec(memory_space=pltpu.VMEM)
    return pl.pallas_call(
        local_kernel,
        name="local_scores",
        in_specs=[stays] * 7,
        out_specs=[whole] * 7,
        out_shape=[scores, rows, rows, rows, rel, rows, rows],
        scratch_shapes=[
            pltpu.VMEM((seg_rows, width), jnp.bfloat16),
            pltpu.VMEM((1, width), jnp.float32),
            pltpu.VMEM((1, width), jnp.float32),
            pltpu.SemaphoreType.DMA((groups, 3)),
            pltpu.SemaphoreType.DMA((2,)),
            pltpu.SemaphoreType.DMA((2,)),
        ],
        compiler_params=pltpu.CompilerParams(vmem_limit_bytes=VMEM_BYTES),
    )(*map(in_hbm, (queries, keys, rel_keys, values, d_out, bias_u[None], bias_v[None])))


def soft_weights(scores, q_content, key_memory):
    shape = [(scores.shape, jnp.float32)]
    return whole_call(weights_kernel, "soft_weights", shape, scores, q_content, key_memory)[0]


def score_grads(start, span, shared, value_memory):
    weights, q_flipped, keys, values, key_memory, rel_keys, d_out = shared
    seg_count = lax.axis_size("seg")
    pair_count = seg_count // 2
    part_rows = rel_keys.shape[0] // seg_count
    grad = ((span // DH, *weights.shape[1:]), jnp.bfloat16)
    return whole_call(
        functools.partial(scores_kernel, start),
        "score_grads",
        [
            grad,
            grad,
            ((pair_count, part_rows, span), jnp.float32),
            ((pair_count * part_rows + BIAS_ROWS, span), jnp.bfloat16),
            ((2, span), jnp.float32),
        ],
        weights,
        q_flipped,
        keys,
        values,
        key_memory,
        value_memory,
        rel_keys,
        d_out,
    )


def row_grads(grads, grads_rel, q_content, keys, key_memory, rel_keys):
    rows = (keys.shape, jnp.bfloat16)
    operands = *grads, *grads_rel, q_content, keys, key_memory, rel_keys
    kernel = functools.partial(rows_kernel, len(grads))
    return whole_call(kernel, "row_grads", [rows, rows], *operands)


def in_hbm(block):
    return pltpu.with_memory_space_constraint(block, pltpu.HBM)


def from_behind(block, axis):
    count = lax.axis_size(axis)
    return lax.ppermute(block, axis, [(i, (i + 1) % count) for i in range(count)])


def swap(block, axis, flip):
    return lax.ppermute(block, axis, [(i, i ^ flip) for i in range(lax.axis_size(axis))])


def bit_of(axis, flip):
    return (lax.axis_index(axis) // flip) % 2


def split_bias(sums):
    high = sums.astype(jnp.bfloat16)
    return high, (sums - high.astype(jnp.float32)).astype(jnp.bfloat16)


def add_packed(keep, sums, packed):
    rows = keep.shape[0] * keep.shape[1]
    partial = packed[:rows].astype(jnp.float32).reshape(keep.shape)
    halves = packed[rows : rows + 4].astype(jnp.float32)
    return keep + partial, sums + (halves[:2] + halves[2:])


def reduce_by_halves(keeps, sends, sums):
    seg_count = lax.axis_size("seg")
    got = [swap(send, "seg", 1) for send in sends]
    added = [add_packed(*part) for part in zip(keeps, sums, got)]
    partial = jnp.concatenate([part for part, _ in added], 2)
    sums = jnp.concatenate([part for _, part in added], 1)
    part_rows, width = partial.shape[1:]
    flip = 2
    while flip < seg_count:
        parts = partial.reshape(partial.shape[0] // 2, 2, part_rows, width)
        mine = bit_of("seg", flip)
        keep = lax.dynamic_index_in_dim(parts, mine, 1, keepdims=False)
        other = lax.dynamic_index_in_dim(parts, 1 - mine, 1, keepdims=False)
        high, low = split_bias(sums)
        fill = jnp.zeros((BIAS_ROWS - 4, width), jnp.bfloat16)
        packed = jnp.concatenate(
            [other.astype(jnp.bfloat16).reshape(-1, width), high, low, fill], 0
        )
        partial, sums = add_packed(keep, sums, swap(packed, "seg", flip))
        flip *= 2
    partial = partial[0]
    dp_count = lax.axis_size("dp")
    flip = dp_count // 2
    while 2 * flip > DIRECT_PEERS:
        half = partial.shape[1] // 2
        mine = bit_of("dp", flip)
        keep = lax.dynamic_slice_in_dim(partial, mine * half, half, 1)
        other = lax.dynamic_slice_in_dim(partial, (1 - mine) * half, half, 1)
        partial = keep + swap(other.astype(jnp.bfloat16), "dp", flip).astype(jnp.float32)
        sums = sums + swap(sums, "dp", flip)
        flip //= 2
    peers = 2 * flip
    place = lax.axis_index("dp") % peers
    cols = partial.shape[1] // peers
    high, low = split_bias(sums)
    tail = jnp.concatenate([high.reshape(-1, cols), low.reshape(-1, cols)], 0)
    total = lax.dynamic_slice_in_dim(partial, place * cols, cols, 1)
    for distance in range(1, peers):
        other = lax.dynamic_slice_in_dim(partial, (place ^ distance) * cols, cols, 1)
        packed = jnp.concatenate([other.astype(jnp.bfloat16), tail], 0)
        packed = swap(packed, "dp", distance).astype(jnp.float32)
        total = total + packed[:part_rows]
        halves = packed[part_rows:].reshape(2, 2, width)
        sums = sums + (halves[0] + halves[1])
    return total, sums


def split_rows(sums, width):
    rows = [
        sums[row : row + 1, col : col + width]
        for row in range(sums.shape[0])
        for col in range(0, sums.shape[1], width)
    ]
    rows = jnp.concatenate(rows, 0)
    high = rows.astype(jnp.bfloat16).astype(jnp.float32)
    return rows, jnp.concatenate([high, rows - high], 0)


def plane_kernel(chunk_count, *refs):
    keep_refs, got_refs, sum_refs = (refs[n * chunk_count : (n + 1) * chunk_count] for n in range(3))
    own_ref, sums_ref, send_y_ref, send_x_ref, send_xy_ref = refs[3 * chunk_count :]
    part_rows, width = own_ref.shape
    upper = lax.axis_index("seg") // 2 == 1
    right = lax.axis_index("dp") % 2 == 1
    cols = 2 * width // lax.axis_size("dp")
    starts = [sum(ref.shape[1] for ref in sum_refs[:n]) for n in range(chunk_count)]

    def columns(start):
        chunk = max(n for n in range(chunk_count) if starts[n] <= start)
        at = slice(start - starts[chunk], start - starts[chunk] + cols)
        parts = []
        for part in range(2):
            rows = slice(part * part_rows, (part + 1) * part_rows)
            parts.append(keep_refs[chunk][part, :, at] + got_refs[chunk][rows, at].astype(jnp.float32))
        return jnp.where(upper, parts[1], parts[0]), jnp.where(upper, parts[0], parts[1])

    for pair in range(lax.axis_size("dp") // 2):
        mine_left, other_left = columns(2 * pair * cols)
        mine_right, other_right = columns((2 * pair + 1) * cols)
        at = slice(pair * cols, (pair + 1) * cols)
        rows = slice(0, part_rows)
        own_ref[:, at] = jnp.where(right, mine_right, mine_left)
        send_x_ref[rows, at] = jnp.where(right, mine_left, mine_right).astype(jnp.bfloat16)
        send_y_ref[rows, at] = jnp.where(right, other_right, other_left).astype(jnp.bfloat16)
        send_xy_ref[rows, at] = jnp.where(right, other_left, other_right).astype(jnp.bfloat16)
    halves = [ref[2 * part_rows : 2 * part_rows + 4].astype(jnp.float32) for ref in got_refs]
    sums = [ref[...] + (half[:2] + half[2:]) for ref, half in zip(sum_refs, halves)]
    sums, tail = split_rows(jnp.concatenate(sums, 1), width)
    sums_ref[...] = sums
    for ref in (send_y_ref, send_x_ref, send_xy_ref):
        ref[part_rows:, :] = tail.astype(jnp.bfloat16)


def line_kernel(own_ref, sums_ref, *refs):
    got_refs, (total_ref, rows_ref, *send_refs) = refs[:3], refs[3:]
    part_rows, cols = total_ref.shape
    place = lax.axis_index("dp") // 2
    count = own_ref.shape[1] // cols
    blocks = []
    for n in range(count):
        at = slice(n * cols, (n + 1) * cols)
        block = own_ref[:, at]
        for ref in got_refs:
            block = block + ref[:part_rows, at].astype(jnp.float32)
        blocks.append(block)
    sums = sums_ref[...]
    for ref in got_refs:
        halves = ref[part_rows:, :].astype(jnp.float32)
        sums = sums + (halves[: sums.shape[0]] + halves[sums.shape[0] :])
    lanes = cols // 2
    half = sums.shape[0] // 2
    rows = []
    for side in (sums[:half], sums[half:]):
        pieces = [
            side[row : row + 1, col : col + lanes]
            for row in range(half)
            for col in range(0, side.shape[1], lanes)
        ]
        rows.append(jnp.concatenate(pieces, 0))
    rows = jnp.concatenate(rows, 1)
    rows_ref[...] = rows
    for distance, ref in zip(range(count), (total_ref, *send_refs)):
        block = blocks[distance]
        for n in range(1, count):
            block = jnp.where(place == n, blocks[n ^ distance], block)
        if distance == 0:
            ref[...] = block
        else:
            ref[:part_rows, :] = block.astype(jnp.bfloat16)
            ref[part_rows:, :] = rows.astype(jnp.bfloat16)


def last_kernel(total_ref, rows_ref, *refs):
    got_refs, (out_ref, bias_u_ref, bias_v_ref) = refs[:-3], refs[-3:]
    part_rows, cols = total_ref.shape
    total, rows = total_ref[...], rows_ref[...]
    for ref in got_refs:
        total = total + ref[:part_rows, :].astype(jnp.float32)
        rows = rows + ref[part_rows:, :].astype(jnp.float32)
    out_ref[...] = total
    bias_u_ref[...] = rows[:, : cols // 2]
    bias_v_ref[...] = rows[:, cols // 2 :]


def whole_call(kernel, name, out_shape, *operands):
    return pl.pallas_call(
        kernel,
        name=name,
        out_shape=[jax.ShapeDtypeStruct(*shape) for shape in out_shape],
        compiler_params=pltpu.CompilerParams(vmem_limit_bytes=VMEM_BYTES),
    )(*operands)


def reduce_by_planes(keeps, sends, sums):
    dp_count = lax.axis_size("dp")
    got = [swap(send, "seg", 1) for send in sends]
    part_rows = keeps[0].shape[1]
    width = sum(keep.shape[2] for keep in keeps)
    half = width // 2
    tail = 2 * 2 * width // half
    send = ((part_rows + tail, half), jnp.bfloat16)
    own, plane_sums, *sends = whole_call(
        functools.partial(plane_kernel, len(keeps)),
        "plane_parts",
        [((part_rows, half), jnp.float32), ((tail // 2, half), jnp.float32), send, send, send],
        *keeps,
        *got,
        *sums,
    )
    got = [
        swap_both(sends[2], 2, 1),
        swap_both(sends[0], 2, 0),
        swap_both(sends[1], 0, 1),
    ]
    cols = width // dp_count
    tail = 2 * width // cols
    send = ((part_rows + tail, cols), jnp.bfloat16)
    peers = dp_count // 2
    total, rows, *sends = whole_call(
        line_kernel,
        "line_parts",
        [((part_rows, cols), jnp.float32), ((tail, cols), jnp.float32)] + [send] * (peers - 1),
        own,
        plane_sums,
        *got,
    )
    got = [swap(sends[distance - 1], "dp", 2 * distance) for distance in (2, 3, 1)]
    side = ((tail, cols // 2), jnp.float32)
    total, *sums = whole_call(
        last_kernel, "last_sums", [((part_rows, cols), jnp.float32), side, side], total, rows, *got
    )
    return total, [half.reshape(width) for half in sums]


def swap_both(block, seg_flip, dp_flip):
    dp_count = lax.axis_size("dp")
    route = [
        (s * dp_count + d, (s ^ seg_flip) * dp_count + (d ^ dp_flip))
        for s in range(lax.axis_size("seg"))
        for d in range(dp_count)
    ]
    return lax.ppermute(block, ("seg", "dp"), route)


def shards(queries, keys, values, rel_keys, bias_u, bias_v, d_out):
    seg_rows, width = queries.shape[1:]
    mem_len = rel_keys.shape[0] - seg_rows
    edges = [(sum(CHUNKS[:n]), span) for n, span in enumerate(CHUNKS)]
    key_memory = from_behind(keys[0, seg_rows - mem_len :], "seg")
    value_memory = [
        from_behind(values[0, seg_rows - mem_len :, start : start + span], "seg")
        for start, span in edges
    ]
    scores, q_content, q_flipped, own_k, rel_keys, own_v, own_d = local_scores(
        queries[0], keys[0], rel_keys, values[0], d_out[0], bias_u, bias_v
    )
    weights = soft_weights(scores, q_content, key_memory)
    shared = weights, q_flipped, own_k, own_v, key_memory, rel_keys, own_d
    parts = [
        score_grads(start, span, shared, block) for (start, span), block in zip(edges, value_memory)
    ]
    grads, grads_rel, keeps, sends, sums = zip(*parts)
    planes = lax.axis_size("seg") == 4 and lax.axis_size("dp") == 8
    reduce = reduce_by_planes if planes else reduce_by_halves
    total, sums = reduce(keeps, sends, sums)
    d_query, d_key = row_grads(grads, grads_rel, q_content, own_k, key_memory, rel_keys)
    return (d_query[None], d_key[None], total, sums[0], sums[1])


def solution(mesh):
    placed = (
        P("dp", "seg", None),
        P("dp", "seg", None),
        P("dp", "seg", None),
        P(),
        P(),
        P(),
        P("dp", "seg", None),
    )
    return jax.shard_map(
        shards,
        mesh=mesh,
        in_specs=placed,
        out_specs=(P("dp", "seg", None), P("dp", "seg", None), P("seg", "dp"), P(), P()),
        check_vma=False,
    )
```

```python
import functools

import jax
import jax.numpy as jnp
from jax import lax
from jax.experimental import pallas as pl
from jax.experimental.pallas import tpu as pltpu
from jax.sharding import PartitionSpec as P

DH = 128
LOG2_E = 1.4426950408889634
GROUP = 4
CHUNKS = (768, 768, 512)
VMEM_BYTES = 24 * 1024 * 1024
SCORE_SCALE = DH ** (-0.5)
BIAS_ROWS = 8
DIRECT_PEERS = 8


def contract(left, right, left_dim, right_dim):
    return lax.dot_general(
        left,
        right,
        (((left_dim,), (right_dim,)), ((), ())),
        preferred_element_type=jnp.float32,
    )


def local_kernel(
    q_hbm,
    k_hbm,
    rel_hbm,
    v_hbm,
    d_out_hbm,
    bias_u_hbm,
    bias_v_hbm,
    score_ref,
    content_ref,
    flipped_ref,
    k_ref,
    rel_ref,
    v_ref,
    d_out_ref,
    q_ref,
    bias_u_ref,
    bias_v_ref,
    head_sems,
    bias_sems,
    rest_sems,
):
    seg_rows, width = q_ref.shape
    key_count = rel_ref.shape[0]
    mem_len = key_count - seg_rows
    groups = head_groups(0, width)
    pairs = (q_hbm, q_ref), (rel_hbm, rel_ref), (k_hbm, k_ref)
    biases = [
        pltpu.make_async_copy(bias_u_hbm, bias_u_ref, bias_sems.at[0]),
        pltpu.make_async_copy(bias_v_hbm, bias_v_ref, bias_sems.at[1]),
    ]
    copies = []
    for n, group in enumerate(groups):
        span = pl.ds(group[0] * DH, len(group) * DH)
        copies.append(
            [
                pltpu.make_async_copy(src.at[:, span], dst.at[:, span], head_sems.at[n, at])
                for at, (src, dst) in enumerate(pairs)
            ]
        )
    rest = [
        pltpu.make_async_copy(v_hbm, v_ref, rest_sems.at[0]),
        pltpu.make_async_copy(d_out_hbm, d_out_ref, rest_sems.at[1]),
    ]
    copies[0] = biases + copies[0]
    for copy in [each for part in copies for each in part] + rest:
        copy.start()
    first_key = jnp.where(lax.axis_index("seg") > 0, 0, mem_len)
    row_index = lax.broadcasted_iota(jnp.int32, (seg_rows, key_count), 0)
    key_index = lax.broadcasted_iota(jnp.int32, (seg_rows, key_count), 1)
    allowed = (key_index <= row_index + mem_len) & (key_index >= first_key)
    flip = row_flip(seg_rows)
    for group, part in zip(groups, copies):
        for copy in part:
            copy.wait()
        cols = columns_of(group)
        n = range(len(cols))
        wide = [q_ref[:, c].astype(jnp.float32) for c in cols]
        q_position = [(wide[t] + bias_v_ref[:, cols[t]]).astype(jnp.bfloat16) for t in n]
        by_distance = [contract(q_position[t], rel_ref[:, cols[t]], 1, 1) for t in n]
        q_content = [(wide[t] + bias_u_ref[:, cols[t]]).astype(jnp.bfloat16) for t in n]
        content = [contract(q_content[t], k_ref[:, cols[t]], 1, 1) for t in n]
        flipped = [contract(flip, q_position[t], 1, 0).astype(jnp.bfloat16) for t in n]
        position = [
            pltpu.roll(raw, key_count - seg_rows + 1, 1, stride=1, stride_axis=0)
            for raw in by_distance
        ]
        for t in n:
            scores = jnp.concatenate(
                [position[t][:, :mem_len], position[t][:, mem_len:] + content[t]], 1
            )
            score_ref[group[t]] = jnp.where(allowed, SCORE_SCALE * LOG2_E * scores, -1e30)
            content_ref[:, cols[t]] = q_content[t]
            flipped_ref[:, cols[t]] = flipped[t]
    for copy in rest:
        copy.wait()


def weights_kernel(score_ref, content_ref, k_mem_ref, weights_ref):
    mem_len = k_mem_ref.shape[0]
    for group in head_groups(0, content_ref.shape[1]):
        cols = columns_of(group)
        n = range(len(cols))
        content = [contract(content_ref[:, c], k_mem_ref[:, c], 1, 1) for c in cols]
        left = [score_ref[group[t], :, :mem_len] + SCORE_SCALE * LOG2_E * content[t] for t in n]
        scores = [jnp.concatenate([left[t], score_ref[group[t], :, mem_len:]], 1) for t in n]
        top = [jnp.max(score, axis=1, keepdims=True) for score in scores]
        raised = [jnp.exp2(scores[t] - top[t]) for t in n]
        total = [jnp.sum(each, axis=1, keepdims=True) for each in raised]
        for t in n:
            weights_ref[group[t]] = raised[t] * (SCORE_SCALE / total[t])


def scores_kernel(
    start,
    weights_ref,
    flipped_ref,
    k_ref,
    v_ref,
    k_mem_ref,
    v_mem_ref,
    rel_ref,
    d_out_ref,
    grad_ref,
    grad_rel_ref,
    keep_ref,
    send_ref,
    bias_ref,
):
    seg_rows = k_ref.shape[0]
    pair_count, part_rows, _ = keep_ref.shape
    odd = jnp.bitwise_and(lax.axis_index("seg"), 1) == 1
    flip = row_flip(seg_rows)
    fill = jnp.zeros((BIAS_ROWS - 4, DH), jnp.bfloat16)
    for group in head_groups(start, v_mem_ref.shape[1]):
        cols = columns_of(group)
        own = columns_of(group, start)
        n = range(len(cols))
        values_all = [
            jnp.concatenate([v_mem_ref[:, own[t]], v_ref[:, cols[t]]], 0) for t in n
        ]
        d_weights = [contract(d_out_ref[:, cols[t]], values_all[t], 1, 1) for t in n]
        scaled = [weights_ref[group[t]] * d_weights[t] for t in n]
        mean = [jnp.sum(each, axis=1, keepdims=True) * (1.0 / SCORE_SCALE) for each in scaled]
        grad = [(weights_ref[group[t]] * (d_weights[t] - mean[t])).astype(jnp.bfloat16) for t in n]
        flipped = [contract(flip, each, 1, 0) for each in grad]
        rolled = [pltpu.roll(each, 0, 1, stride=1, stride_axis=0) for each in flipped]
        grad_rel = [each.astype(jnp.bfloat16) for each in rolled]
        d_rel_all = [contract(grad_rel[t], flipped_ref[:, cols[t]], 0, 0) for t in n]
        keys_all = [jnp.concatenate([k_mem_ref[:, c], k_ref[:, c]], 0) for c in cols]
        content = [row_sum_product(flipped[t], keys_all[t]) for t in n]
        position = [row_sum_product(rolled[t], rel_ref[:, cols[t]]) for t in n]
        for t in n:
            c = own[t]
            grad_ref[group[t] - start // DH] = grad[t]
            grad_rel_ref[group[t] - start // DH] = grad_rel[t]
            sums = jnp.concatenate([content[t], position[t]], 0)
            bias_ref[:, c] = sums
            high, low = split_bias(sums)
            d_rel = d_rel_all[t]
            for pair in range(pair_count):
                at = 2 * pair * part_rows
                even_part = d_rel[at : at + part_rows]
                odd_part = d_rel[at + part_rows : at + 2 * part_rows]
                keep_ref[pair, :, c] = jnp.where(odd, odd_part, even_part)
                send_ref[pair * part_rows : (pair + 1) * part_rows, c] = jnp.where(
                    odd, even_part, odd_part
                ).astype(jnp.bfloat16)
            send_ref[pair_count * part_rows :, c] = jnp.concatenate([high, low, fill], 0)


def row_sum_product(left, right):
    rest = jnp.sum(left, 0, keepdims=True)
    parts = []
    for _ in range(3):
        part = rest.astype(jnp.bfloat16)
        rest = rest - part.astype(jnp.float32)
        parts.append(part)
    fill = jnp.zeros((5, left.shape[1]), jnp.bfloat16)
    return jnp.sum(contract(jnp.concatenate([*parts, fill], 0), right, 1, 0), 0, keepdims=True)


def rows_kernel(chunk_count, *refs):
    grad_refs, grad_rel_refs = refs[:chunk_count], refs[chunk_count : 2 * chunk_count]
    content_ref, k_ref, k_mem_ref, rel_ref, d_q_ref, d_k_ref = refs[2 * chunk_count :]
    mem_len = k_mem_ref.shape[0]
    flip = row_flip(k_ref.shape[0])
    heads = [(n, head) for n, ref in enumerate(grad_refs) for head in range(ref.shape[0])]
    for group in head_groups(0, k_ref.shape[1]):
        cols = columns_of(group)
        places = [heads[head] for head in group]
        n = range(len(cols))
        grad = [grad_refs[chunk][head] for chunk, head in places]
        back = [
            contract(flip, grad_rel_refs[chunk][head], 1, 0).astype(jnp.bfloat16)
            for chunk, head in places
        ]
        keys_all = [jnp.concatenate([k_mem_ref[:, c], k_ref[:, c]], 0) for c in cols]
        d_content = [contract(grad[t], keys_all[t], 1, 0) for t in n]
        d_key = [contract(grad[t][:, mem_len:], content_ref[:, cols[t]], 0, 0) for t in n]
        d_position = [contract(back[t], rel_ref[:, cols[t]], 1, 0) for t in n]
        for t in n:
            d_q_ref[:, cols[t]] = (d_content[t] + d_position[t]).astype(jnp.bfloat16)
            d_k_ref[:, cols[t]] = d_key[t].astype(jnp.bfloat16)


def row_flip(rows):
    row = lax.broadcasted_iota(jnp.int32, (rows, rows), 0)
    col = lax.broadcasted_iota(jnp.int32, (rows, rows), 1)
    return (row + col == rows - 1).astype(jnp.bfloat16)


def head_groups(start, span):
    heads = range(start // DH, (start + span) // DH)
    size = GROUP if len(heads) % GROUP == 0 else len(heads)
    return [heads[at : at + size] for at in range(0, len(heads), size)]


def columns_of(heads, start=0):
    return [slice(head * DH - start, (head + 1) * DH - start) for head in heads]


def local_scores(queries, keys, rel_keys, values, d_out, bias_u, bias_v):
    seg_rows, width = queries.shape
    rows = jax.ShapeDtypeStruct((seg_rows, width), jnp.bfloat16)
    groups = len(head_groups(0, width))
    scores = jax.ShapeDtypeStruct((width // DH, seg_rows, rel_keys.shape[0]), jnp.float32)
    rel = jax.ShapeDtypeStruct(rel_keys.shape, jnp.bfloat16)
    stays = pl.BlockSpec(memory_space=pl.ANY)
    whole = pl.BlockSpec(memory_space=pltpu.VMEM)
    return pl.pallas_call(
        local_kernel,
        name="local_scores",
        in_specs=[stays] * 7,
        out_specs=[whole] * 7,
        out_shape=[scores, rows, rows, rows, rel, rows, rows],
        scratch_shapes=[
            pltpu.VMEM((seg_rows, width), jnp.bfloat16),
            pltpu.VMEM((1, width), jnp.float32),
            pltpu.VMEM((1, width), jnp.float32),
            pltpu.SemaphoreType.DMA((groups, 3)),
            pltpu.SemaphoreType.DMA((2,)),
            pltpu.SemaphoreType.DMA((2,)),
        ],
        compiler_params=pltpu.CompilerParams(vmem_limit_bytes=VMEM_BYTES),
    )(*map(in_hbm, (queries, keys, rel_keys, values, d_out, bias_u[None], bias_v[None])))


def soft_weights(scores, q_content, key_memory):
    shape = [(scores.shape, jnp.float32)]
    return whole_call(weights_kernel, "soft_weights", shape, scores, q_content, key_memory)[0]


def score_grads(start, span, shared, value_memory):
    weights, q_flipped, keys, values, key_memory, rel_keys, d_out = shared
    seg_count = lax.axis_size("seg")
    pair_count = seg_count // 2
    part_rows = rel_keys.shape[0] // seg_count
    grad = ((span // DH, *weights.shape[1:]), jnp.bfloat16)
    return whole_call(
        functools.partial(scores_kernel, start),
        "score_grads",
        [
            grad,
            grad,
            ((pair_count, part_rows, span), jnp.float32),
            ((pair_count * part_rows + BIAS_ROWS, span), jnp.bfloat16),
            ((2, span), jnp.float32),
        ],
        weights,
        q_flipped,
        keys,
        values,
        key_memory,
        value_memory,
        rel_keys,
        d_out,
    )


def row_grads(grads, grads_rel, q_content, keys, key_memory, rel_keys):
    rows = (keys.shape, jnp.bfloat16)
    operands = *grads, *grads_rel, q_content, keys, key_memory, rel_keys
    kernel = functools.partial(rows_kernel, len(grads))
    return whole_call(kernel, "row_grads", [rows, rows], *operands)


def in_hbm(block):
    return pltpu.with_memory_space_constraint(block, pltpu.HBM)


def from_behind(block, axis):
    count = lax.axis_size(axis)
    return lax.ppermute(block, axis, [(i, (i + 1) % count) for i in range(count)])


def swap(block, axis, flip):
    return lax.ppermute(block, axis, [(i, i ^ flip) for i in range(lax.axis_size(axis))])


def bit_of(axis, flip):
    return (lax.axis_index(axis) // flip) % 2


def split_bias(sums):
    high = sums.astype(jnp.bfloat16)
    return high, (sums - high.astype(jnp.float32)).astype(jnp.bfloat16)


def add_packed(keep, sums, packed):
    rows = keep.shape[0] * keep.shape[1]
    partial = packed[:rows].astype(jnp.float32).reshape(keep.shape)
    halves = packed[rows : rows + 4].astype(jnp.float32)
    return keep + partial, sums + (halves[:2] + halves[2:])


def reduce_by_halves(keeps, sends, sums, row_operands):
    seg_count = lax.axis_size("seg")
    got = [swap(send, "seg", 1) for send in sends]
    added = [add_packed(*part) for part in zip(keeps, sums, got)]
    partial = jnp.concatenate([part for part, _ in added], 2)
    sums = jnp.concatenate([part for _, part in added], 1)
    part_rows, width = partial.shape[1:]
    flip = 2
    while flip < seg_count:
        parts = partial.reshape(partial.shape[0] // 2, 2, part_rows, width)
        mine = bit_of("seg", flip)
        keep = lax.dynamic_index_in_dim(parts, mine, 1, keepdims=False)
        other = lax.dynamic_index_in_dim(parts, 1 - mine, 1, keepdims=False)
        high, low = split_bias(sums)
        fill = jnp.zeros((BIAS_ROWS - 4, width), jnp.bfloat16)
        packed = jnp.concatenate(
            [other.astype(jnp.bfloat16).reshape(-1, width), high, low, fill], 0
        )
        partial, sums = add_packed(keep, sums, swap(packed, "seg", flip))
        flip *= 2
    partial = partial[0]
    dp_count = lax.axis_size("dp")
    flip = dp_count // 2
    while 2 * flip > DIRECT_PEERS:
        half = partial.shape[1] // 2
        mine = bit_of("dp", flip)
        keep = lax.dynamic_slice_in_dim(partial, mine * half, half, 1)
        other = lax.dynamic_slice_in_dim(partial, (1 - mine) * half, half, 1)
        partial = keep + swap(other.astype(jnp.bfloat16), "dp", flip).astype(jnp.float32)
        sums = sums + swap(sums, "dp", flip)
        flip //= 2
    peers = 2 * flip
    place = lax.axis_index("dp") % peers
    cols = partial.shape[1] // peers
    high, low = split_bias(sums)
    tail = jnp.concatenate([high.reshape(-1, cols), low.reshape(-1, cols)], 0)
    total = lax.dynamic_slice_in_dim(partial, place * cols, cols, 1)
    for distance in range(1, peers):
        other = lax.dynamic_slice_in_dim(partial, (place ^ distance) * cols, cols, 1)
        packed = jnp.concatenate([other.astype(jnp.bfloat16), tail], 0)
        packed = swap(packed, "dp", distance).astype(jnp.float32)
        total = total + packed[:part_rows]
        halves = packed[part_rows:].reshape(2, 2, width)
        sums = sums + (halves[0] + halves[1])
    return total, sums, row_grads(*row_operands)


def side_by_side(sums):
    sides = []
    for row in range(sums.shape[0]):
        pieces = [sums[row : row + 1, at : at + DH] for at in range(0, sums.shape[1], DH)]
        sides.append(jnp.concatenate(pieces, 0))
    return jnp.concatenate(sides, 1)


def plane_kernel(chunk_count, *refs):
    keep_refs, got_refs, sum_refs = (refs[n * chunk_count : (n + 1) * chunk_count] for n in range(3))
    own_ref, sums_ref, send_y_ref, send_x_ref, send_xy_ref = refs[3 * chunk_count :]
    part_rows = keep_refs[0].shape[1]
    cols = own_ref.shape[1]
    upper = lax.axis_index("seg") // 2 == 1
    right = lax.axis_index("dp") % 2 == 1
    starts = [sum(ref.shape[1] for ref in sum_refs[:n]) for n in range(chunk_count)]

    def columns(start):
        chunk = max(n for n in range(chunk_count) if starts[n] <= start)
        at = slice(start - starts[chunk], start - starts[chunk] + cols)
        parts = []
        for part in range(2):
            rows = slice(part * part_rows, (part + 1) * part_rows)
            parts.append(keep_refs[chunk][part, :, at] + got_refs[chunk][rows, at].astype(jnp.float32))
        return jnp.where(upper, parts[1], parts[0]), jnp.where(upper, parts[0], parts[1])

    for pair in range(lax.axis_size("dp") // 2):
        mine_left, other_left = columns(2 * pair * cols)
        mine_right, other_right = columns((2 * pair + 1) * cols)
        rows = slice(pair * part_rows, (pair + 1) * part_rows)
        own_ref[rows] = jnp.where(right, mine_right, mine_left)
        send_x_ref[rows] = jnp.where(right, mine_left, mine_right).astype(jnp.bfloat16)
        send_y_ref[rows] = jnp.where(right, other_right, other_left).astype(jnp.bfloat16)
        send_xy_ref[rows] = jnp.where(right, other_left, other_right).astype(jnp.bfloat16)
    halves = [ref[2 * part_rows : 2 * part_rows + 4].astype(jnp.float32) for ref in got_refs]
    sums = [ref[...] + (half[:2] + half[2:]) for ref, half in zip(sum_refs, halves)]
    rows = side_by_side(jnp.concatenate(sums, 1))
    sums_ref[...] = rows
    for ref in (send_y_ref, send_x_ref, send_xy_ref):
        ref[own_ref.shape[0] :] = rows.astype(jnp.bfloat16)


def line_kernel(own_ref, sums_ref, *refs):
    got_refs, (total_ref, rows_ref, *send_refs) = refs[:3], refs[3:]
    part_rows, cols = total_ref.shape
    place = lax.axis_index("dp") // 2
    count = own_ref.shape[0] // part_rows
    blocks = []
    for n in range(count):
        at = slice(n * part_rows, (n + 1) * part_rows)
        block = own_ref[at]
        for ref in got_refs:
            block = block + ref[at].astype(jnp.float32)
        blocks.append(block)
    rows = sums_ref[...]
    for ref in got_refs:
        rows = rows + ref[own_ref.shape[0] :].astype(jnp.float32)
    rows_ref[...] = rows
    for distance, ref in zip(range(count), (total_ref, *send_refs)):
        block = blocks[distance]
        for n in range(1, count):
            block = jnp.where(place == n, blocks[n ^ distance], block)
        if distance == 0:
            ref[...] = block
        else:
            ref[:part_rows, :] = block.astype(jnp.bfloat16)
            ref[part_rows:, :] = rows.astype(jnp.bfloat16)


def last_kernel(total_ref, rows_ref, *refs):
    got_refs, (out_ref, bias_u_ref, bias_v_ref) = refs[:-3], refs[-3:]
    part_rows, cols = total_ref.shape
    total, rows = total_ref[...], rows_ref[...]
    for ref in got_refs:
        total = total + ref[:part_rows, :].astype(jnp.float32)
        rows = rows + ref[part_rows:, :].astype(jnp.float32)
    out_ref[...] = total
    bias_u_ref[...] = rows[:, : cols // 2]
    bias_v_ref[...] = rows[:, cols // 2 :]


def whole_call(kernel, name, out_shape, *operands):
    return pl.pallas_call(
        kernel,
        name=name,
        out_shape=[jax.ShapeDtypeStruct(*shape) for shape in out_shape],
        compiler_params=pltpu.CompilerParams(vmem_limit_bytes=VMEM_BYTES),
    )(*operands)


def reduce_by_planes(keeps, sends, sums, row_operands):
    dp_count = lax.axis_size("dp")
    got = [swap(send, "seg", 1) for send in sends]
    part_rows = keeps[0].shape[1]
    width = sum(keep.shape[2] for keep in keeps)
    cols = width // dp_count
    peers = dp_count // 2
    tail = width // DH
    own_rows = peers * part_rows
    send = ((own_rows + tail, cols), jnp.bfloat16)
    own, plane_sums, *sends = whole_call(
        functools.partial(plane_kernel, len(keeps)),
        "plane_parts",
        [((own_rows, cols), jnp.float32), ((tail, cols), jnp.float32), send, send, send],
        *keeps,
        *got,
        *sums,
    )
    own, row_operands = lax.optimization_barrier((own, row_operands))
    rows = row_grads(*row_operands)
    got = [
        swap_both(sends[2], 2, 1),
        swap_both(sends[0], 2, 0),
        swap_both(sends[1], 0, 1),
    ]
    own, rows = lax.optimization_barrier((own, rows))
    send = ((part_rows + tail, cols), jnp.bfloat16)
    total, bias_rows, *sends = whole_call(
        line_kernel,
        "line_parts",
        [((part_rows, cols), jnp.float32), ((tail, cols), jnp.float32)] + [send] * (peers - 1),
        own,
        plane_sums,
        *got,
    )
    got = [swap(sends[distance - 1], "dp", 2 * distance) for distance in (2, 3, 1)]
    side = ((tail, cols // 2), jnp.float32)
    total, *sums = whole_call(
        last_kernel, "last_sums", [((part_rows, cols), jnp.float32), side, side], total, bias_rows, *got
    )
    return total, [half.reshape(width) for half in sums], rows


def swap_both(block, seg_flip, dp_flip):
    dp_count = lax.axis_size("dp")
    route = [
        (s * dp_count + d, (s ^ seg_flip) * dp_count + (d ^ dp_flip))
        for s in range(lax.axis_size("seg"))
        for d in range(dp_count)
    ]
    return lax.ppermute(block, ("seg", "dp"), route)


def shards(queries, keys, values, rel_keys, bias_u, bias_v, d_out):
    seg_rows, width = queries.shape[1:]
    mem_len = rel_keys.shape[0] - seg_rows
    edges = [(sum(CHUNKS[:n]), span) for n, span in enumerate(CHUNKS)]
    key_memory = from_behind(keys[0, seg_rows - mem_len :], "seg")
    value_memory = [
        from_behind(values[0, seg_rows - mem_len :, start : start + span], "seg")
        for start, span in edges
    ]
    scores, q_content, q_flipped, own_k, rel_keys, own_v, own_d = local_scores(
        queries[0], keys[0], rel_keys, values[0], d_out[0], bias_u, bias_v
    )
    weights = soft_weights(scores, q_content, key_memory)
    shared = weights, q_flipped, own_k, own_v, key_memory, rel_keys, own_d
    parts = [
        score_grads(start, span, shared, block) for (start, span), block in zip(edges, value_memory)
    ]
    grads, grads_rel, keeps, sends, sums = zip(*parts)
    cols = width // lax.axis_size("dp")
    planes = lax.axis_size("seg") == 4 and lax.axis_size("dp") == 8 and cols == 2 * DH
    reduce = reduce_by_planes if planes else reduce_by_halves
    row_operands = grads, grads_rel, q_content, own_k, key_memory, rel_keys
    total, sums, (d_query, d_key) = reduce(keeps, sends, sums, row_operands)
    return (d_query[None], d_key[None], total, sums[0], sums[1])


def solution(mesh):
    placed = (
        P("dp", "seg", None),
        P("dp", "seg", None),
        P("dp", "seg", None),
        P(),
        P(),
        P(),
        P("dp", "seg", None),
    )
    return jax.shard_map(
        shards,
        mesh=mesh,
        in_specs=placed,
        out_specs=(P("dp", "seg", None), P("dp", "seg", None), P("seg", "dp"), P(), P()),
        check_vma=False,
    )
```

```python
import functools

import jax
import jax.numpy as jnp
from jax import lax
from jax.experimental import pallas as pl
from jax.experimental.pallas import tpu as pltpu
from jax.sharding import PartitionSpec as P

DH = 128
LOG2_E = 1.4426950408889634
GROUP = 4
CHUNKS = (768, 768, 512)
VMEM_BYTES = 24 * 1024 * 1024
SCORE_SCALE = DH ** (-0.5)
BIAS_ROWS = 8
DIRECT_PEERS = 8


def contract(left, right, left_dim, right_dim):
    return lax.dot_general(
        left,
        right,
        (((left_dim,), (right_dim,)), ((), ())),
        preferred_element_type=jnp.float32,
    )


def local_kernel(
    q_hbm,
    k_hbm,
    rel_hbm,
    v_hbm,
    d_out_hbm,
    bias_u_hbm,
    bias_v_hbm,
    score_ref,
    content_ref,
    flipped_ref,
    k_ref,
    rel_ref,
    v_ref,
    d_out_ref,
    q_ref,
    d_raw_ref,
    bias_u_ref,
    bias_v_ref,
    head_sems,
    bias_sems,
    rest_sems,
):
    seg_rows, width = q_ref.shape
    key_count = rel_ref.shape[0]
    mem_len = key_count - seg_rows
    groups = head_groups(0, width)
    pairs = (q_hbm, q_ref), (rel_hbm, rel_ref), (k_hbm, k_ref)
    biases = [
        pltpu.make_async_copy(bias_u_hbm, bias_u_ref, bias_sems.at[0]),
        pltpu.make_async_copy(bias_v_hbm, bias_v_ref, bias_sems.at[1]),
    ]
    copies = []
    for n, group in enumerate(groups):
        span = pl.ds(group[0] * DH, len(group) * DH)
        copies.append(
            [
                pltpu.make_async_copy(src.at[:, span], dst.at[:, span], head_sems.at[n, at])
                for at, (src, dst) in enumerate(pairs)
            ]
        )
    rest = [
        pltpu.make_async_copy(v_hbm, v_ref, rest_sems.at[0]),
        pltpu.make_async_copy(d_out_hbm, d_raw_ref, rest_sems.at[1]),
    ]
    copies[0] = biases + copies[0]
    for copy in [each for part in copies for each in part] + rest:
        copy.start()
    first_key = jnp.where(lax.axis_index("seg") > 0, 0, mem_len)
    row_index = lax.broadcasted_iota(jnp.int32, (seg_rows, key_count), 0)
    key_index = lax.broadcasted_iota(jnp.int32, (seg_rows, key_count), 1)
    allowed = (row_index + key_index < key_count) & (key_index >= first_key)
    flip = row_flip(seg_rows)
    for group, part in zip(groups, copies):
        for copy in part:
            copy.wait()
        cols = columns_of(group)
        n = range(len(cols))
        wide = [q_ref[:, c].astype(jnp.float32) for c in cols]
        q_position = [(wide[t] + bias_v_ref[:, cols[t]]).astype(jnp.bfloat16) for t in n]
        by_distance = [contract(q_position[t], rel_ref[:, cols[t]], 1, 1) for t in n]
        q_content = [(wide[t] + bias_u_ref[:, cols[t]]).astype(jnp.bfloat16) for t in n]
        q_content = [contract(flip, each, 1, 0).astype(jnp.bfloat16) for each in q_content]
        content = [contract(q_content[t], k_ref[:, cols[t]], 1, 1) for t in n]
        q_position = [contract(flip, each, 1, 0).astype(jnp.bfloat16) for each in q_position]
        position = [
            pltpu.roll(raw, key_count - seg_rows + 1, 1, stride=1, stride_axis=0)
            for raw in by_distance
        ]
        position = [flip_exactly(flip, each) for each in position]
        for t in n:
            scores = jnp.concatenate(
                [position[t][:, :mem_len], position[t][:, mem_len:] + content[t]], 1
            )
            score_ref[group[t]] = jnp.where(allowed, SCORE_SCALE * LOG2_E * scores, -1e30)
            content_ref[:, cols[t]] = q_content[t]
            flipped_ref[:, cols[t]] = q_position[t]
    for copy in rest:
        copy.wait()
    d_out_ref[...] = contract(flip, d_raw_ref[...], 1, 0).astype(jnp.bfloat16)


def bf16_parts(wide):
    parts = []
    for _ in range(3):
        part = wide.astype(jnp.bfloat16)
        wide = wide - part.astype(jnp.float32)
        parts.append(part)
    return parts


def flip_exactly(flip, wide):
    high, middle, low = (contract(flip, part, 1, 0) for part in bf16_parts(wide))
    return (high + middle) + low


def weights_kernel(score_ref, content_ref, k_mem_ref, weights_ref):
    mem_len = k_mem_ref.shape[0]
    for group in head_groups(0, content_ref.shape[1]):
        cols = columns_of(group)
        n = range(len(cols))
        content = [contract(content_ref[:, c], k_mem_ref[:, c], 1, 1) for c in cols]
        left = [score_ref[group[t], :, :mem_len] + SCORE_SCALE * LOG2_E * content[t] for t in n]
        scores = [jnp.concatenate([left[t], score_ref[group[t], :, mem_len:]], 1) for t in n]
        top = [jnp.max(score, axis=1, keepdims=True) for score in scores]
        raised = [jnp.exp2(scores[t] - top[t]) for t in n]
        total = [jnp.sum(each, axis=1, keepdims=True) for each in raised]
        for t in n:
            weights_ref[group[t]] = raised[t] * (SCORE_SCALE / total[t])


def scores_kernel(
    start,
    weights_ref,
    flipped_ref,
    k_ref,
    v_ref,
    k_mem_ref,
    v_mem_ref,
    rel_ref,
    d_out_ref,
    grad_ref,
    grad_rel_ref,
    keep_ref,
    send_ref,
    bias_ref,
):
    pair_count, part_rows, _ = keep_ref.shape
    odd = jnp.bitwise_and(lax.axis_index("seg"), 1) == 1
    fill = jnp.zeros((BIAS_ROWS - 4, DH), jnp.bfloat16)
    for group in head_groups(start, v_mem_ref.shape[1]):
        cols = columns_of(group)
        own = columns_of(group, start)
        n = range(len(cols))
        values_all = [
            jnp.concatenate([v_mem_ref[:, own[t]], v_ref[:, cols[t]]], 0) for t in n
        ]
        d_weights = [contract(d_out_ref[:, cols[t]], values_all[t], 1, 1) for t in n]
        scaled = [weights_ref[group[t]] * d_weights[t] for t in n]
        mean = [jnp.sum(each, axis=1, keepdims=True) * (1.0 / SCORE_SCALE) for each in scaled]
        grad = [(weights_ref[group[t]] * (d_weights[t] - mean[t])).astype(jnp.bfloat16) for t in n]
        grad_wide = [each.astype(jnp.float32) for each in grad]
        rolled = [pltpu.roll(each, 0, 1, stride=1, stride_axis=0) for each in grad_wide]
        grad_rel = [each.astype(jnp.bfloat16) for each in rolled]
        d_rel_all = [contract(grad_rel[t], flipped_ref[:, cols[t]], 0, 0) for t in n]
        keys_all = [jnp.concatenate([k_mem_ref[:, c], k_ref[:, c]], 0) for c in cols]
        content = [row_sum_product(grad_wide[t], keys_all[t]) for t in n]
        position = [row_sum_product(rolled[t], rel_ref[:, cols[t]]) for t in n]
        for t in n:
            c = own[t]
            grad_ref[group[t] - start // DH] = grad[t]
            grad_rel_ref[group[t] - start // DH] = grad_rel[t]
            sums = jnp.concatenate([content[t], position[t]], 0)
            bias_ref[:, c] = sums
            high, low = split_bias(sums)
            d_rel = d_rel_all[t]
            for pair in range(pair_count):
                at = 2 * pair * part_rows
                even_part = d_rel[at : at + part_rows]
                odd_part = d_rel[at + part_rows : at + 2 * part_rows]
                keep_ref[pair, :, c] = jnp.where(odd, odd_part, even_part)
                send_ref[pair * part_rows : (pair + 1) * part_rows, c] = jnp.where(
                    odd, even_part, odd_part
                ).astype(jnp.bfloat16)
            send_ref[pair_count * part_rows :, c] = jnp.concatenate([high, low, fill], 0)


def row_sum_product(left, right):
    parts = bf16_parts(jnp.sum(left, 0, keepdims=True))
    fill = jnp.zeros((5, left.shape[1]), jnp.bfloat16)
    return jnp.sum(contract(jnp.concatenate([*parts, fill], 0), right, 1, 0), 0, keepdims=True)


def rows_kernel(chunk_count, *refs):
    grad_refs, grad_rel_refs = refs[:chunk_count], refs[chunk_count : 2 * chunk_count]
    content_ref, k_ref, k_mem_ref, rel_ref, d_q_ref, d_k_ref = refs[2 * chunk_count :]
    mem_len = k_mem_ref.shape[0]
    flip = row_flip(k_ref.shape[0])
    heads = [(n, head) for n, ref in enumerate(grad_refs) for head in range(ref.shape[0])]
    for group in head_groups(0, k_ref.shape[1]):
        cols = columns_of(group)
        places = [heads[head] for head in group]
        n = range(len(cols))
        grad = [grad_refs[chunk][head] for chunk, head in places]
        grad_rel = [grad_rel_refs[chunk][head] for chunk, head in places]
        keys_all = [jnp.concatenate([k_mem_ref[:, c], k_ref[:, c]], 0) for c in cols]
        d_content = [contract(grad[t], keys_all[t], 1, 0) for t in n]
        d_key = [contract(grad[t][:, mem_len:], content_ref[:, cols[t]], 0, 0) for t in n]
        d_position = [contract(grad_rel[t], rel_ref[:, cols[t]], 1, 0) for t in n]
        d_query = [(d_content[t] + d_position[t]).astype(jnp.bfloat16) for t in n]
        for t in n:
            d_q_ref[:, cols[t]] = contract(flip, d_query[t], 1, 0).astype(jnp.bfloat16)
            d_k_ref[:, cols[t]] = d_key[t].astype(jnp.bfloat16)


def row_flip(rows):
    row = lax.broadcasted_iota(jnp.int32, (rows, rows), 0)
    col = lax.broadcasted_iota(jnp.int32, (rows, rows), 1)
    return (row + col == rows - 1).astype(jnp.bfloat16)


def head_groups(start, span):
    heads = range(start // DH, (start + span) // DH)
    size = GROUP if len(heads) % GROUP == 0 else len(heads)
    return [heads[at : at + size] for at in range(0, len(heads), size)]


def columns_of(heads, start=0):
    return [slice(head * DH - start, (head + 1) * DH - start) for head in heads]


def local_scores(queries, keys, rel_keys, values, d_out, bias_u, bias_v):
    seg_rows, width = queries.shape
    rows = jax.ShapeDtypeStruct((seg_rows, width), jnp.bfloat16)
    groups = len(head_groups(0, width))
    scores = jax.ShapeDtypeStruct((width // DH, seg_rows, rel_keys.shape[0]), jnp.float32)
    rel = jax.ShapeDtypeStruct(rel_keys.shape, jnp.bfloat16)
    stays = pl.BlockSpec(memory_space=pl.ANY)
    whole = pl.BlockSpec(memory_space=pltpu.VMEM)
    return pl.pallas_call(
        local_kernel,
        name="local_scores",
        in_specs=[stays] * 7,
        out_specs=[whole] * 7,
        out_shape=[scores, rows, rows, rows, rel, rows, rows],
        scratch_shapes=[
            pltpu.VMEM((seg_rows, width), jnp.bfloat16),
            pltpu.VMEM((seg_rows, width), jnp.bfloat16),
            pltpu.VMEM((1, width), jnp.float32),
            pltpu.VMEM((1, width), jnp.float32),
            pltpu.SemaphoreType.DMA((groups, 3)),
            pltpu.SemaphoreType.DMA((2,)),
            pltpu.SemaphoreType.DMA((2,)),
        ],
        compiler_params=pltpu.CompilerParams(vmem_limit_bytes=VMEM_BYTES),
    )(*map(in_hbm, (queries, keys, rel_keys, values, d_out, bias_u[None], bias_v[None])))


def soft_weights(scores, q_content, key_memory):
    shape = [(scores.shape, jnp.float32)]
    return whole_call(weights_kernel, "soft_weights", shape, scores, q_content, key_memory)[0]


def score_grads(start, span, shared, value_memory):
    weights, q_flipped, keys, values, key_memory, rel_keys, d_out = shared
    seg_count = lax.axis_size("seg")
    pair_count = seg_count // 2
    part_rows = rel_keys.shape[0] // seg_count
    grad = ((span // DH, *weights.shape[1:]), jnp.bfloat16)
    return whole_call(
        functools.partial(scores_kernel, start),
        "score_grads",
        [
            grad,
            grad,
            ((pair_count, part_rows, span), jnp.float32),
            ((pair_count * part_rows + BIAS_ROWS, span), jnp.bfloat16),
            ((2, span), jnp.float32),
        ],
        weights,
        q_flipped,
        keys,
        values,
        key_memory,
        value_memory,
        rel_keys,
        d_out,
    )


def row_grads(grads, grads_rel, q_content, keys, key_memory, rel_keys):
    rows = (keys.shape, jnp.bfloat16)
    operands = *grads, *grads_rel, q_content, keys, key_memory, rel_keys
    kernel = functools.partial(rows_kernel, len(grads))
    return whole_call(kernel, "row_grads", [rows, rows], *operands)


def in_hbm(block):
    return pltpu.with_memory_space_constraint(block, pltpu.HBM)


def from_behind(block, axis):
    count = lax.axis_size(axis)
    return lax.ppermute(block, axis, [(i, (i + 1) % count) for i in range(count)])


def swap(block, axis, flip):
    return lax.ppermute(block, axis, [(i, i ^ flip) for i in range(lax.axis_size(axis))])


def bit_of(axis, flip):
    return (lax.axis_index(axis) // flip) % 2


def split_bias(sums):
    high = sums.astype(jnp.bfloat16)
    return high, (sums - high.astype(jnp.float32)).astype(jnp.bfloat16)


def add_packed(keep, sums, packed):
    rows = keep.shape[0] * keep.shape[1]
    partial = packed[:rows].astype(jnp.float32).reshape(keep.shape)
    halves = packed[rows : rows + 4].astype(jnp.float32)
    return keep + partial, sums + (halves[:2] + halves[2:])


def reduce_by_halves(keeps, sends, sums, row_operands):
    seg_count = lax.axis_size("seg")
    got = [swap(send, "seg", 1) for send in sends]
    added = [add_packed(*part) for part in zip(keeps, sums, got)]
    partial = jnp.concatenate([part for part, _ in added], 2)
    sums = jnp.concatenate([part for _, part in added], 1)
    part_rows, width = partial.shape[1:]
    flip = 2
    while flip < seg_count:
        parts = partial.reshape(partial.shape[0] // 2, 2, part_rows, width)
        mine = bit_of("seg", flip)
        keep = lax.dynamic_index_in_dim(parts, mine, 1, keepdims=False)
        other = lax.dynamic_index_in_dim(parts, 1 - mine, 1, keepdims=False)
        high, low = split_bias(sums)
        fill = jnp.zeros((BIAS_ROWS - 4, width), jnp.bfloat16)
        packed = jnp.concatenate(
            [other.astype(jnp.bfloat16).reshape(-1, width), high, low, fill], 0
        )
        partial, sums = add_packed(keep, sums, swap(packed, "seg", flip))
        flip *= 2
    partial = partial[0]
    dp_count = lax.axis_size("dp")
    flip = dp_count // 2
    while 2 * flip > DIRECT_PEERS:
        half = partial.shape[1] // 2
        mine = bit_of("dp", flip)
        keep = lax.dynamic_slice_in_dim(partial, mine * half, half, 1)
        other = lax.dynamic_slice_in_dim(partial, (1 - mine) * half, half, 1)
        partial = keep + swap(other.astype(jnp.bfloat16), "dp", flip).astype(jnp.float32)
        sums = sums + swap(sums, "dp", flip)
        flip //= 2
    peers = 2 * flip
    place = lax.axis_index("dp") % peers
    cols = partial.shape[1] // peers
    high, low = split_bias(sums)
    tail = jnp.concatenate([high.reshape(-1, cols), low.reshape(-1, cols)], 0)
    total = lax.dynamic_slice_in_dim(partial, place * cols, cols, 1)
    for distance in range(1, peers):
        other = lax.dynamic_slice_in_dim(partial, (place ^ distance) * cols, cols, 1)
        packed = jnp.concatenate([other.astype(jnp.bfloat16), tail], 0)
        packed = swap(packed, "dp", distance).astype(jnp.float32)
        total = total + packed[:part_rows]
        halves = packed[part_rows:].reshape(2, 2, width)
        sums = sums + (halves[0] + halves[1])
    return total, sums, row_grads(*row_operands)


def side_by_side(sums):
    sides = []
    for row in range(sums.shape[0]):
        pieces = [sums[row : row + 1, at : at + DH] for at in range(0, sums.shape[1], DH)]
        sides.append(jnp.concatenate(pieces, 0))
    return jnp.concatenate(sides, 1)


def plane_kernel(chunk_count, *refs):
    keep_refs, got_refs, sum_refs = (refs[n * chunk_count : (n + 1) * chunk_count] for n in range(3))
    own_ref, sums_ref, send_y_ref, send_x_ref, send_xy_ref = refs[3 * chunk_count :]
    part_rows = keep_refs[0].shape[1]
    cols = own_ref.shape[1]
    upper = lax.axis_index("seg") // 2 == 1
    right = lax.axis_index("dp") % 2 == 1
    starts = [sum(ref.shape[1] for ref in sum_refs[:n]) for n in range(chunk_count)]

    def columns(start):
        chunk = max(n for n in range(chunk_count) if starts[n] <= start)
        at = slice(start - starts[chunk], start - starts[chunk] + cols)
        parts = []
        for part in range(2):
            rows = slice(part * part_rows, (part + 1) * part_rows)
            parts.append(keep_refs[chunk][part, :, at] + got_refs[chunk][rows, at].astype(jnp.float32))
        return jnp.where(upper, parts[1], parts[0]), jnp.where(upper, parts[0], parts[1])

    for pair in range(lax.axis_size("dp") // 2):
        mine_left, other_left = columns(2 * pair * cols)
        mine_right, other_right = columns((2 * pair + 1) * cols)
        rows = slice(pair * part_rows, (pair + 1) * part_rows)
        own_ref[rows] = jnp.where(right, mine_right, mine_left)
        send_x_ref[rows] = jnp.where(right, mine_left, mine_right).astype(jnp.bfloat16)
        send_y_ref[rows] = jnp.where(right, other_right, other_left).astype(jnp.bfloat16)
        send_xy_ref[rows] = jnp.where(right, other_left, other_right).astype(jnp.bfloat16)
    halves = [ref[2 * part_rows : 2 * part_rows + 4].astype(jnp.float32) for ref in got_refs]
    sums = [ref[...] + (half[:2] + half[2:]) for ref, half in zip(sum_refs, halves)]
    rows = side_by_side(jnp.concatenate(sums, 1))
    sums_ref[...] = rows
    for ref in (send_y_ref, send_x_ref, send_xy_ref):
        ref[own_ref.shape[0] :] = rows.astype(jnp.bfloat16)


def line_kernel(own_ref, sums_ref, *refs):
    got_refs, (total_ref, rows_ref, *send_refs) = refs[:3], refs[3:]
    part_rows, cols = total_ref.shape
    place = lax.axis_index("dp") // 2
    count = own_ref.shape[0] // part_rows
    blocks = []
    for n in range(count):
        at = slice(n * part_rows, (n + 1) * part_rows)
        block = own_ref[at]
        for ref in got_refs:
            block = block + ref[at].astype(jnp.float32)
        blocks.append(block)
    rows = sums_ref[...]
    for ref in got_refs:
        rows = rows + ref[own_ref.shape[0] :].astype(jnp.float32)
    rows_ref[...] = rows
    for distance, ref in zip(range(count), (total_ref, *send_refs)):
        block = blocks[distance]
        for n in range(1, count):
            block = jnp.where(place == n, blocks[n ^ distance], block)
        if distance == 0:
            ref[...] = block
        else:
            ref[:part_rows, :] = block.astype(jnp.bfloat16)
            ref[part_rows:, :] = rows.astype(jnp.bfloat16)


def last_kernel(total_ref, rows_ref, *refs):
    got_refs, (out_ref, bias_u_ref, bias_v_ref) = refs[:-3], refs[-3:]
    part_rows, cols = total_ref.shape
    total, rows = total_ref[...], rows_ref[...]
    for ref in got_refs:
        total = total + ref[:part_rows, :].astype(jnp.float32)
        rows = rows + ref[part_rows:, :].astype(jnp.float32)
    out_ref[...] = total
    bias_u_ref[...] = rows[:, : cols // 2]
    bias_v_ref[...] = rows[:, cols // 2 :]


def whole_call(kernel, name, out_shape, *operands):
    return pl.pallas_call(
        kernel,
        name=name,
        out_shape=[jax.ShapeDtypeStruct(*shape) for shape in out_shape],
        compiler_params=pltpu.CompilerParams(vmem_limit_bytes=VMEM_BYTES),
    )(*operands)


def reduce_by_planes(keeps, sends, sums, row_operands):
    dp_count = lax.axis_size("dp")
    got = [swap(send, "seg", 1) for send in sends]
    part_rows = keeps[0].shape[1]
    width = sum(keep.shape[2] for keep in keeps)
    cols = width // dp_count
    peers = dp_count // 2
    tail = width // DH
    own_rows = peers * part_rows
    send = ((own_rows + tail, cols), jnp.bfloat16)
    own, plane_sums, *sends = whole_call(
        functools.partial(plane_kernel, len(keeps)),
        "plane_parts",
        [((own_rows, cols), jnp.float32), ((tail, cols), jnp.float32), send, send, send],
        *keeps,
        *got,
        *sums,
    )
    own, row_operands = lax.optimization_barrier((own, row_operands))
    rows = row_grads(*row_operands)
    got = [
        swap_both(sends[2], 2, 1),
        swap_both(sends[0], 2, 0),
        swap_both(sends[1], 0, 1),
    ]
    own, rows = lax.optimization_barrier((own, rows))
    send = ((part_rows + tail, cols), jnp.bfloat16)
    total, bias_rows, *sends = whole_call(
        line_kernel,
        "line_parts",
        [((part_rows, cols), jnp.float32), ((tail, cols), jnp.float32)] + [send] * (peers - 1),
        own,
        plane_sums,
        *got,
    )
    got = [swap(sends[distance - 1], "dp", 2 * distance) for distance in (2, 3, 1)]
    side = ((tail, cols // 2), jnp.float32)
    total, *sums = whole_call(
        last_kernel, "last_sums", [((part_rows, cols), jnp.float32), side, side], total, bias_rows, *got
    )
    return total, [half.reshape(width) for half in sums], rows


def swap_both(block, seg_flip, dp_flip):
    dp_count = lax.axis_size("dp")
    route = [
        (s * dp_count + d, (s ^ seg_flip) * dp_count + (d ^ dp_flip))
        for s in range(lax.axis_size("seg"))
        for d in range(dp_count)
    ]
    return lax.ppermute(block, ("seg", "dp"), route)


def shards(queries, keys, values, rel_keys, bias_u, bias_v, d_out):
    seg_rows, width = queries.shape[1:]
    mem_len = rel_keys.shape[0] - seg_rows
    edges = [(sum(CHUNKS[:n]), span) for n, span in enumerate(CHUNKS)]
    key_memory = from_behind(keys[0, seg_rows - mem_len :], "seg")
    value_memory = [
        from_behind(values[0, seg_rows - mem_len :, start : start + span], "seg")
        for start, span in edges
    ]
    scores, q_content, q_flipped, own_k, rel_keys, own_v, own_d = local_scores(
        queries[0], keys[0], rel_keys, values[0], d_out[0], bias_u, bias_v
    )
    weights = soft_weights(scores, q_content, key_memory)
    shared = weights, q_flipped, own_k, own_v, key_memory, rel_keys, own_d
    parts = [
        score_grads(start, span, shared, block) for (start, span), block in zip(edges, value_memory)
    ]
    grads, grads_rel, keeps, sends, sums = zip(*parts)
    cols = width // lax.axis_size("dp")
    planes = lax.axis_size("seg") == 4 and lax.axis_size("dp") == 8 and cols == 2 * DH
    reduce = reduce_by_planes if planes else reduce_by_halves
    row_operands = grads, grads_rel, q_content, own_k, key_memory, rel_keys
    total, sums, (d_query, d_key) = reduce(keeps, sends, sums, row_operands)
    return (d_query[None], d_key[None], total, sums[0], sums[1])


def solution(mesh):
    placed = (
        P("dp", "seg", None),
        P("dp", "seg", None),
        P("dp", "seg", None),
        P(),
        P(),
        P(),
        P("dp", "seg", None),
    )
    return jax.shard_map(
        shards,
        mesh=mesh,
        in_specs=placed,
        out_specs=(P("dp", "seg", None), P("dp", "seg", None), P("seg", "dp"), P(), P()),
        check_vma=False,
    )
```

```python
import functools

import jax
import jax.numpy as jnp
from jax import lax
from jax.experimental import pallas as pl
from jax.experimental.pallas import tpu as pltpu
from jax.sharding import PartitionSpec as P

DH = 128
LOG2_E = 1.4426950408889634
GROUP = 4
CHUNKS = (768, 768, 512)
VMEM_BYTES = 24 * 1024 * 1024
SCORE_SCALE = DH ** (-0.5)
BIAS_ROWS = 8
DIRECT_PEERS = 8


def contract(left, right, left_dim, right_dim):
    return lax.dot_general(
        left,
        right,
        (((left_dim,), (right_dim,)), ((), ())),
        preferred_element_type=jnp.float32,
    )


def local_kernel(
    q_hbm,
    k_hbm,
    rel_hbm,
    v_hbm,
    d_out_hbm,
    bias_u_hbm,
    bias_v_hbm,
    score_ref,
    content_ref,
    flipped_ref,
    k_ref,
    rel_ref,
    v_ref,
    d_out_ref,
    q_ref,
    d_raw_ref,
    bias_u_ref,
    bias_v_ref,
    head_sems,
    bias_sems,
    rest_sems,
):
    seg_rows, width = q_ref.shape
    key_count = rel_ref.shape[0]
    mem_len = key_count - seg_rows
    groups = head_groups(0, width)
    pairs = (q_hbm, q_ref), (rel_hbm, rel_ref), (k_hbm, k_ref)
    biases = [
        pltpu.make_async_copy(bias_u_hbm, bias_u_ref, bias_sems.at[0]),
        pltpu.make_async_copy(bias_v_hbm, bias_v_ref, bias_sems.at[1]),
    ]
    copies = []
    for n, group in enumerate(groups):
        span = pl.ds(group[0] * DH, len(group) * DH)
        copies.append(
            [
                pltpu.make_async_copy(src.at[:, span], dst.at[:, span], head_sems.at[n, at])
                for at, (src, dst) in enumerate(pairs)
            ]
        )
    rest = [
        pltpu.make_async_copy(v_hbm, v_ref, rest_sems.at[0]),
        pltpu.make_async_copy(d_out_hbm, d_raw_ref, rest_sems.at[1]),
    ]
    copies[0] = biases + copies[0]
    for copy in [each for part in copies for each in part] + rest:
        copy.start()
    first_key = jnp.where(lax.axis_index("seg") > 0, 0, mem_len)
    row_index = lax.broadcasted_iota(jnp.int32, (seg_rows, key_count), 0)
    key_index = lax.broadcasted_iota(jnp.int32, (seg_rows, key_count), 1)
    allowed = (row_index + key_index < key_count) & (key_index >= first_key)
    flip = row_flip(seg_rows)
    for group, part in zip(groups, copies):
        for copy in part:
            copy.wait()
        cols = columns_of(group)
        n = range(len(cols))
        wide = [q_ref[:, c].astype(jnp.float32) for c in cols]
        q_position = [(wide[t] + bias_v_ref[:, cols[t]]).astype(jnp.bfloat16) for t in n]
        by_distance = [contract(q_position[t], rel_ref[:, cols[t]], 1, 1) for t in n]
        q_content = [(wide[t] + bias_u_ref[:, cols[t]]).astype(jnp.bfloat16) for t in n]
        q_content = [contract(flip, each, 1, 0).astype(jnp.bfloat16) for each in q_content]
        content = [contract(q_content[t], k_ref[:, cols[t]], 1, 1) for t in n]
        q_position = [contract(flip, each, 1, 0).astype(jnp.bfloat16) for each in q_position]
        position = [
            pltpu.roll(raw, key_count - seg_rows + 1, 1, stride=1, stride_axis=0)
            for raw in by_distance
        ]
        position = [flip_exactly(flip, each) for each in position]
        for t in n:
            scores = jnp.concatenate(
                [position[t][:, :mem_len], position[t][:, mem_len:] + content[t]], 1
            )
            score_ref[group[t]] = jnp.where(allowed, SCORE_SCALE * LOG2_E * scores, -1e30)
            content_ref[:, cols[t]] = q_content[t]
            flipped_ref[:, cols[t]] = q_position[t]
    for copy in rest:
        copy.wait()
    d_out_ref[...] = contract(flip, d_raw_ref[...], 1, 0).astype(jnp.bfloat16)


def bf16_parts(wide):
    parts = []
    for _ in range(3):
        part = wide.astype(jnp.bfloat16)
        wide = wide - part.astype(jnp.float32)
        parts.append(part)
    return parts


def flip_exactly(flip, wide):
    high, middle, low = (contract(flip, part, 1, 0) for part in bf16_parts(wide))
    return (high + middle) + low


def weights_kernel(score_ref, content_ref, k_mem_ref, weights_ref):
    mem_len = k_mem_ref.shape[0]
    for group in head_groups(0, content_ref.shape[1]):
        cols = columns_of(group)
        n = range(len(cols))
        content = [contract(content_ref[:, c], k_mem_ref[:, c], 1, 1) for c in cols]
        left = [score_ref[group[t], :, :mem_len] + SCORE_SCALE * LOG2_E * content[t] for t in n]
        scores = [jnp.concatenate([left[t], score_ref[group[t], :, mem_len:]], 1) for t in n]
        top = [jnp.max(score, axis=1, keepdims=True) for score in scores]
        raised = [jnp.exp2(scores[t] - top[t]) for t in n]
        total = [jnp.sum(each, axis=1, keepdims=True) for each in raised]
        for t in n:
            weights_ref[group[t]] = raised[t] * (SCORE_SCALE / total[t])


def scores_kernel(
    start,
    weights_ref,
    flipped_ref,
    k_ref,
    v_ref,
    k_mem_ref,
    v_mem_ref,
    rel_ref,
    d_out_ref,
    grad_ref,
    grad_rel_ref,
    keep_ref,
    send_ref,
    bias_ref,
):
    pair_count, part_rows, _ = keep_ref.shape
    odd = jnp.bitwise_and(lax.axis_index("seg"), 1) == 1
    fill = jnp.zeros((BIAS_ROWS - 4, DH), jnp.bfloat16)
    for group in head_groups(start, v_mem_ref.shape[1]):
        cols = columns_of(group)
        own = columns_of(group, start)
        n = range(len(cols))
        values_all = [
            jnp.concatenate([v_mem_ref[:, own[t]], v_ref[:, cols[t]]], 0) for t in n
        ]
        d_weights = [contract(d_out_ref[:, cols[t]], values_all[t], 1, 1) for t in n]
        scaled = [weights_ref[group[t]] * d_weights[t] for t in n]
        mean = [jnp.sum(each, axis=1, keepdims=True) * (1.0 / SCORE_SCALE) for each in scaled]
        grad = [(weights_ref[group[t]] * (d_weights[t] - mean[t])).astype(jnp.bfloat16) for t in n]
        grad_wide = [each.astype(jnp.float32) for each in grad]
        rolled = [pltpu.roll(each, 0, 1, stride=1, stride_axis=0) for each in grad_wide]
        grad_rel = [each.astype(jnp.bfloat16) for each in rolled]
        d_rel_all = [contract(grad_rel[t], flipped_ref[:, cols[t]], 0, 0) for t in n]
        keys_all = [jnp.concatenate([k_mem_ref[:, c], k_ref[:, c]], 0) for c in cols]
        content = [row_sum_product(grad_wide[t], keys_all[t]) for t in n]
        position = [row_sum_product(rolled[t], rel_ref[:, cols[t]]) for t in n]
        for t in n:
            c = own[t]
            grad_ref[group[t] - start // DH] = grad[t]
            grad_rel_ref[group[t] - start // DH] = grad_rel[t]
            sums = jnp.concatenate([content[t], position[t]], 0)
            bias_ref[:, c] = sums
            high, low = split_bias(sums)
            d_rel = d_rel_all[t]
            for pair in range(pair_count):
                at = 2 * pair * part_rows
                even_part = d_rel[at : at + part_rows]
                odd_part = d_rel[at + part_rows : at + 2 * part_rows]
                keep_ref[pair, :, c] = jnp.where(odd, odd_part, even_part)
                send_ref[pair * part_rows : (pair + 1) * part_rows, c] = jnp.where(
                    odd, even_part, odd_part
                ).astype(jnp.bfloat16)
            send_ref[pair_count * part_rows :, c] = jnp.concatenate([high, low, fill], 0)


def row_sum_product(left, right):
    parts = bf16_parts(jnp.sum(left, 0, keepdims=True))
    fill = jnp.zeros((5, left.shape[1]), jnp.bfloat16)
    return jnp.sum(contract(jnp.concatenate([*parts, fill], 0), right, 1, 0), 0, keepdims=True)


def rows_kernel(chunk_count, *refs):
    grad_refs, grad_rel_refs = refs[:chunk_count], refs[chunk_count : 2 * chunk_count]
    content_ref, k_ref, k_mem_ref, rel_ref, d_q_ref, d_k_ref = refs[2 * chunk_count :]
    mem_len = k_mem_ref.shape[0]
    flip = row_flip(k_ref.shape[0])
    heads = [(n, head) for n, ref in enumerate(grad_refs) for head in range(ref.shape[0])]
    for group in head_groups(0, k_ref.shape[1]):
        cols = columns_of(group)
        places = [heads[head] for head in group]
        n = range(len(cols))
        grad = [grad_refs[chunk][head] for chunk, head in places]
        grad_rel = [grad_rel_refs[chunk][head] for chunk, head in places]
        keys_all = [jnp.concatenate([k_mem_ref[:, c], k_ref[:, c]], 0) for c in cols]
        d_content = [contract(grad[t], keys_all[t], 1, 0) for t in n]
        d_key = [contract(grad[t][:, mem_len:], content_ref[:, cols[t]], 0, 0) for t in n]
        d_position = [contract(grad_rel[t], rel_ref[:, cols[t]], 1, 0) for t in n]
        d_query = [(d_content[t] + d_position[t]).astype(jnp.bfloat16) for t in n]
        for t in n:
            d_q_ref[:, cols[t]] = contract(flip, d_query[t], 1, 0).astype(jnp.bfloat16)
            d_k_ref[:, cols[t]] = d_key[t].astype(jnp.bfloat16)


def row_flip(rows):
    row = lax.broadcasted_iota(jnp.int32, (rows, rows), 0)
    col = lax.broadcasted_iota(jnp.int32, (rows, rows), 1)
    return (row + col == rows - 1).astype(jnp.bfloat16)


def head_groups(start, span):
    heads = range(start // DH, (start + span) // DH)
    size = GROUP if len(heads) % GROUP == 0 else len(heads)
    return [heads[at : at + size] for at in range(0, len(heads), size)]


def columns_of(heads, start=0):
    return [slice(head * DH - start, (head + 1) * DH - start) for head in heads]


def local_scores(queries, keys, rel_keys, values, d_out, bias_u, bias_v):
    seg_rows, width = queries.shape
    rows = jax.ShapeDtypeStruct((seg_rows, width), jnp.bfloat16)
    groups = len(head_groups(0, width))
    scores = jax.ShapeDtypeStruct((width // DH, seg_rows, rel_keys.shape[0]), jnp.float32)
    rel = jax.ShapeDtypeStruct(rel_keys.shape, jnp.bfloat16)
    stays = pl.BlockSpec(memory_space=pl.ANY)
    whole = pl.BlockSpec(memory_space=pltpu.VMEM)
    return pl.pallas_call(
        local_kernel,
        name="local_scores",
        in_specs=[stays] * 7,
        out_specs=[whole] * 7,
        out_shape=[scores, rows, rows, rows, rel, rows, rows],
        scratch_shapes=[
            pltpu.VMEM((seg_rows, width), jnp.bfloat16),
            pltpu.VMEM((seg_rows, width), jnp.bfloat16),
            pltpu.VMEM((1, width), jnp.float32),
            pltpu.VMEM((1, width), jnp.float32),
            pltpu.SemaphoreType.DMA((groups, 3)),
            pltpu.SemaphoreType.DMA((2,)),
            pltpu.SemaphoreType.DMA((2,)),
        ],
        compiler_params=pltpu.CompilerParams(vmem_limit_bytes=VMEM_BYTES),
    )(*map(in_hbm, (queries, keys, rel_keys, values, d_out, bias_u[None], bias_v[None])))


def soft_weights(scores, q_content, key_memory):
    shape = [(scores.shape, jnp.float32)]
    return whole_call(weights_kernel, "soft_weights", shape, scores, q_content, key_memory)[0]


def score_grads(start, span, shared, value_memory):
    weights, q_flipped, keys, values, key_memory, rel_keys, d_out = shared
    seg_count = lax.axis_size("seg")
    pair_count = seg_count // 2
    part_rows = rel_keys.shape[0] // seg_count
    grad = ((span // DH, *weights.shape[1:]), jnp.bfloat16)
    return whole_call(
        functools.partial(scores_kernel, start),
        "score_grads",
        [
            grad,
            grad,
            ((pair_count, part_rows, span), jnp.float32),
            ((pair_count * part_rows + BIAS_ROWS, span), jnp.bfloat16),
            ((2, span), jnp.float32),
        ],
        weights,
        q_flipped,
        keys,
        values,
        key_memory,
        value_memory,
        rel_keys,
        d_out,
    )


def row_grads(grads, grads_rel, q_content, keys, key_memory, rel_keys):
    rows = (keys.shape, jnp.bfloat16)
    operands = *grads, *grads_rel, q_content, keys, key_memory, rel_keys
    kernel = functools.partial(rows_kernel, len(grads))
    return whole_call(kernel, "row_grads", [rows, rows], *operands)


def in_hbm(block):
    return pltpu.with_memory_space_constraint(block, pltpu.HBM)


def from_behind(block, axis):
    count = lax.axis_size(axis)
    return lax.ppermute(block, axis, [(i, (i + 1) % count) for i in range(count)])


def swap(block, axis, flip):
    return lax.ppermute(block, axis, [(i, i ^ flip) for i in range(lax.axis_size(axis))])


def bit_of(axis, flip):
    return (lax.axis_index(axis) // flip) % 2


def split_bias(sums):
    high = sums.astype(jnp.bfloat16)
    return high, (sums - high.astype(jnp.float32)).astype(jnp.bfloat16)


def add_packed(keep, sums, packed):
    rows = keep.shape[0] * keep.shape[1]
    partial = packed[:rows].astype(jnp.float32).reshape(keep.shape)
    halves = packed[rows : rows + 4].astype(jnp.float32)
    return keep + partial, sums + (halves[:2] + halves[2:])


def reduce_by_halves(keeps, sends, sums, row_operands):
    seg_count = lax.axis_size("seg")
    got = [swap(send, "seg", 1) for send in sends]
    added = [add_packed(*part) for part in zip(keeps, sums, got)]
    partial = jnp.concatenate([part for part, _ in added], 2)
    sums = jnp.concatenate([part for _, part in added], 1)
    part_rows, width = partial.shape[1:]
    flip = 2
    while flip < seg_count:
        parts = partial.reshape(partial.shape[0] // 2, 2, part_rows, width)
        mine = bit_of("seg", flip)
        keep = lax.dynamic_index_in_dim(parts, mine, 1, keepdims=False)
        other = lax.dynamic_index_in_dim(parts, 1 - mine, 1, keepdims=False)
        high, low = split_bias(sums)
        fill = jnp.zeros((BIAS_ROWS - 4, width), jnp.bfloat16)
        packed = jnp.concatenate(
            [other.astype(jnp.bfloat16).reshape(-1, width), high, low, fill], 0
        )
        partial, sums = add_packed(keep, sums, swap(packed, "seg", flip))
        flip *= 2
    partial = partial[0]
    dp_count = lax.axis_size("dp")
    flip = dp_count // 2
    while 2 * flip > DIRECT_PEERS:
        half = partial.shape[1] // 2
        mine = bit_of("dp", flip)
        keep = lax.dynamic_slice_in_dim(partial, mine * half, half, 1)
        other = lax.dynamic_slice_in_dim(partial, (1 - mine) * half, half, 1)
        partial = keep + swap(other.astype(jnp.bfloat16), "dp", flip).astype(jnp.float32)
        sums = sums + swap(sums, "dp", flip)
        flip //= 2
    peers = 2 * flip
    place = lax.axis_index("dp") % peers
    cols = partial.shape[1] // peers
    high, low = split_bias(sums)
    tail = jnp.concatenate([high.reshape(-1, cols), low.reshape(-1, cols)], 0)
    total = lax.dynamic_slice_in_dim(partial, place * cols, cols, 1)
    for distance in range(1, peers):
        other = lax.dynamic_slice_in_dim(partial, (place ^ distance) * cols, cols, 1)
        packed = jnp.concatenate([other.astype(jnp.bfloat16), tail], 0)
        packed = swap(packed, "dp", distance).astype(jnp.float32)
        total = total + packed[:part_rows]
        halves = packed[part_rows:].reshape(2, 2, width)
        sums = sums + (halves[0] + halves[1])
    return total, sums, row_grads(*row_operands)


def side_by_side(sums):
    sides = []
    for row in range(sums.shape[0]):
        pieces = [sums[row : row + 1, at : at + DH] for at in range(0, sums.shape[1], DH)]
        sides.append(jnp.concatenate(pieces, 0))
    return jnp.concatenate(sides, 1)


def plane_kernel(chunk_count, *refs):
    keep_refs, got_refs, sum_refs = (refs[n * chunk_count : (n + 1) * chunk_count] for n in range(3))
    own_ref, sums_ref, send_y_ref, send_x_ref, send_xy_ref = refs[3 * chunk_count :]
    part_rows = keep_refs[0].shape[1]
    cols = own_ref.shape[1]
    upper = lax.axis_index("seg") // 2 == 1
    right = lax.axis_index("dp") % 2 == 1
    starts = [sum(ref.shape[1] for ref in sum_refs[:n]) for n in range(chunk_count)]

    def columns(start):
        chunk = max(n for n in range(chunk_count) if starts[n] <= start)
        at = slice(start - starts[chunk], start - starts[chunk] + cols)
        parts = []
        for part in range(2):
            rows = slice(part * part_rows, (part + 1) * part_rows)
            parts.append(keep_refs[chunk][part, :, at] + got_refs[chunk][rows, at].astype(jnp.float32))
        return jnp.where(upper, parts[1], parts[0]), jnp.where(upper, parts[0], parts[1])

    for pair in range(lax.axis_size("dp") // 2):
        mine_left, other_left = columns(2 * pair * cols)
        mine_right, other_right = columns((2 * pair + 1) * cols)
        rows = slice(pair * part_rows, (pair + 1) * part_rows)
        own_ref[rows] = jnp.where(right, mine_right, mine_left)
        send_x_ref[rows] = jnp.where(right, mine_left, mine_right).astype(jnp.bfloat16)
        send_y_ref[rows] = jnp.where(right, other_right, other_left).astype(jnp.bfloat16)
        send_xy_ref[rows] = jnp.where(right, other_left, other_right).astype(jnp.bfloat16)
    halves = [ref[2 * part_rows : 2 * part_rows + 4].astype(jnp.float32) for ref in got_refs]
    sums = [ref[...] + (half[:2] + half[2:]) for ref, half in zip(sum_refs, halves)]
    rows = side_by_side(jnp.concatenate(sums, 1))
    sums_ref[...] = rows
    for ref in (send_y_ref, send_x_ref, send_xy_ref):
        ref[own_ref.shape[0] :] = rows.astype(jnp.bfloat16)


def line_kernel(own_ref, sums_ref, *refs):
    got_refs, (total_ref, rows_ref, *send_refs) = refs[:3], refs[3:]
    part_rows, cols = total_ref.shape
    place = lax.axis_index("dp") // 2
    count = own_ref.shape[0] // part_rows
    blocks = []
    for n in range(count):
        at = slice(n * part_rows, (n + 1) * part_rows)
        block = own_ref[at]
        for ref in got_refs:
            block = block + ref[at].astype(jnp.float32)
        blocks.append(block)
    rows = sums_ref[...]
    for ref in got_refs:
        rows = rows + ref[own_ref.shape[0] :].astype(jnp.float32)
    rows_ref[...] = rows
    for distance, ref in zip(range(count), (total_ref, *send_refs)):
        block = blocks[distance]
        for n in range(1, count):
            block = jnp.where(place == n, blocks[n ^ distance], block)
        if distance == 0:
            ref[...] = block
        else:
            ref[:part_rows, :] = block.astype(jnp.bfloat16)
            ref[part_rows:, :] = rows.astype(jnp.bfloat16)


def last_kernel(total_ref, rows_ref, *refs):
    got_refs, (out_ref, bias_u_ref, bias_v_ref) = refs[:-3], refs[-3:]
    part_rows, cols = total_ref.shape
    total, rows = total_ref[...], rows_ref[...]
    for ref in got_refs:
        total = total + ref[:part_rows, :].astype(jnp.float32)
        rows = rows + ref[part_rows:, :].astype(jnp.float32)
    out_ref[...] = total
    bias_u_ref[...] = rows[:, : cols // 2]
    bias_v_ref[...] = rows[:, cols // 2 :]


def whole_call(kernel, name, out_shape, *operands):
    return pl.pallas_call(
        kernel,
        name=name,
        out_shape=[jax.ShapeDtypeStruct(*shape) for shape in out_shape],
        compiler_params=pltpu.CompilerParams(vmem_limit_bytes=VMEM_BYTES),
    )(*operands)


def reduce_by_planes(keeps, sends, sums, row_operands):
    dp_count = lax.axis_size("dp")
    got = [swap(send, "seg", 1) for send in sends]
    part_rows = keeps[0].shape[1]
    width = sum(keep.shape[2] for keep in keeps)
    cols = width // dp_count
    peers = dp_count // 2
    tail = width // DH
    own_rows = peers * part_rows
    send = ((own_rows + tail, cols), jnp.bfloat16)
    own, plane_sums, *sends = whole_call(
        functools.partial(plane_kernel, len(keeps)),
        "plane_parts",
        [((own_rows, cols), jnp.float32), ((tail, cols), jnp.float32), send, send, send],
        *keeps,
        *got,
        *sums,
    )
    own, row_operands = lax.optimization_barrier((own, row_operands))
    rows = row_grads(*row_operands)
    got = [
        swap_both(sends[2], 2, 1),
        swap_both(sends[0], 2, 0),
        swap_both(sends[1], 0, 1),
    ]
    own, rows = lax.optimization_barrier((own, rows))
    send = ((part_rows + tail, cols), jnp.bfloat16)
    total, bias_rows, *sends = whole_call(
        line_kernel,
        "line_parts",
        [((part_rows, cols), jnp.float32), ((tail, cols), jnp.float32)] + [send] * (peers - 1),
        own,
        plane_sums,
        *got,
    )
    got = [swap(sends[distance - 1], "dp", 2 * distance) for distance in (3, 2, 1)]
    side = ((tail, cols // 2), jnp.float32)
    total, *sums = whole_call(
        last_kernel, "last_sums", [((part_rows, cols), jnp.float32), side, side], total, bias_rows, *got
    )
    return total, [half.reshape(width) for half in sums], rows


def swap_both(block, seg_flip, dp_flip):
    dp_count = lax.axis_size("dp")
    route = [
        (s * dp_count + d, (s ^ seg_flip) * dp_count + (d ^ dp_flip))
        for s in range(lax.axis_size("seg"))
        for d in range(dp_count)
    ]
    return lax.ppermute(block, ("seg", "dp"), route)


def shards(queries, keys, values, rel_keys, bias_u, bias_v, d_out):
    seg_rows, width = queries.shape[1:]
    mem_len = rel_keys.shape[0] - seg_rows
    edges = [(sum(CHUNKS[:n]), span) for n, span in enumerate(CHUNKS)]
    key_memory = from_behind(keys[0, seg_rows - mem_len :], "seg")
    value_memory = [
        from_behind(values[0, seg_rows - mem_len :, start : start + span], "seg")
        for start, span in edges
    ]
    scores, q_content, q_flipped, own_k, rel_keys, own_v, own_d = local_scores(
        queries[0], keys[0], rel_keys, values[0], d_out[0], bias_u, bias_v
    )
    weights = soft_weights(scores, q_content, key_memory)
    shared = weights, q_flipped, own_k, own_v, key_memory, rel_keys, own_d
    parts = [
        score_grads(start, span, shared, block) for (start, span), block in zip(edges, value_memory)
    ]
    grads, grads_rel, keeps, sends, sums = zip(*parts)
    cols = width // lax.axis_size("dp")
    planes = lax.axis_size("seg") == 4 and lax.axis_size("dp") == 8 and cols == 2 * DH
    reduce = reduce_by_planes if planes else reduce_by_halves
    row_operands = grads, grads_rel, q_content, own_k, key_memory, rel_keys
    total, sums, (d_query, d_key) = reduce(keeps, sends, sums, row_operands)
    return (d_query[None], d_key[None], total, sums[0], sums[1])


def solution(mesh):
    placed = (
        P("dp", "seg", None),
        P("dp", "seg", None),
        P("dp", "seg", None),
        P(),
        P(),
        P(),
        P("dp", "seg", None),
    )
    return jax.shard_map(
        shards,
        mesh=mesh,
        in_specs=placed,
        out_specs=(P("dp", "seg", None), P("dp", "seg", None), P("seg", "dp"), P(), P()),
        check_vma=False,
    )
```
